32 devices in a mesh: row: 8 (over z, core), col: 4 (over y, x).
Axes of the slice: x: 2, y: 2, z: 4, core: 2. Of those that a mesh axis runs over, the one named last changes fastest.
Arguments:
- start_block: bfloat16 [16, 4096], P(None, 'col'), may hold values from -33 to 33
- block_values: bfloat16 [8, 4, 12, 128, 128], P('row', 'col'), may hold values from -0.109375 to 0.109375
- block_columns: int32 [8, 4, 12], P('row', 'col'), may hold values from 0 to 7
- block_counts: int32 [8, 4, 4], P('row', 'col'), may hold values from 1 to 6, 12 in all within a row
Outputs:
- applied_once: bfloat16 [16, 4096], P(None, 'row')
- applied_twice: bfloat16 [16, 4096], P(None, 'row')
- basis_gram: float32 [32, 32], replicated
- projected_gram: float32 [32, 32], replicated
The draws below stay inside these ranges and needn't reach their ends.
All inputs are finite; a program needn't handle non-finite values.
Results may differ from the reference program's by a relative error of at most 0.0039.
Values may be sent and summed in bfloat16 or wider, within the bound.
No kernel may reach another device: no remote copies, remote signals or barrier semaphores. Data moves between devices by JAX's collectives and lax.ppermute only.
A program may use at most 64 MiB of HBM per device.

```python
import math
import jax
import jax.numpy as jnp
import numpy as np
from jax import lax

K = 16
BLK = 128
BLK_MEAN = 3
MOST = 6
NROWB = 4
NCOLB = 8
NNZ = 12
STATES = 4096
N_ROW = 8
N_COL = 4


def draw_start_block(key, part):
    first_key, second_key = jax.random.split(key, 2)
    positions = jnp.arange(STATES, dtype=jnp.float32) / (STATES - 1)
    vector_scales = jnp.exp(jax.random.uniform(second_key, (K, 1), jnp.float32, math.log(0.3), math.log(3.0)))
    values = jnp.clip(jax.random.normal(first_key, (K, STATES), jnp.float32), -4.0, 4.0)
    ramp = jnp.exp(positions * math.log(3.0)) / 1.7
    return (values * vector_scales * ramp).astype(jnp.bfloat16)


def plant(values, stream_key, smallest, high):
    longest = values.shape.index(max(values.shape))
    spots = []
    for shift in (0, 1):
        where = [jax.random.randint(jax.random.fold_in(stream_key, axis), (), 0, length) for axis, length in enumerate(values.shape)]
        where[longest] = (where[longest] + shift) % values.shape[longest]
        spots.append(tuple(where))
    return values.at[spots[0]].set(smallest).at[spots[1]].set(high)


def levels(own_key, dims, shards, least, largest):
    loudness, own = 1.0, jax.random.fold_in(own_key, 6)
    for position, shards_of in shards:
        heights = jnp.exp(jax.random.uniform(jax.random.fold_in(own, position), (shards_of,), jnp.float32, least / len(shards), largest / len(shards)))
        loudness = loudness * jnp.repeat(heights, dims[position] // shards_of).reshape([-1 if axis == position else 1 for axis in range(len(dims))])
    return loudness


def split_up(number_of, total, limit, lean):
    loads = [(1 << 20) // math.isqrt(grade ** lean) + 1 for grade in range(2, number_of + 1)]
    rest, given = total - limit - (number_of - 1), [1] * (number_of - 1)
    while rest > 0:
        candidates = [i for i in range(number_of - 1) if given[i] < limit]
        whole, remaining = sum([loads[i] for i in candidates]), rest
        for i in candidates:
            extra = min(limit - given[i], max(1, remaining * loads[i] // whole), rest)
            given[i] = given[i] + extra
            rest = rest - extra
    return np.array([limit] + given)


def ragged(own_key, number_of, total, reach, lean):
    if number_of == 2:
        one = jax.random.randint(own_key, (), max(1, total - reach), min(reach, total - 1) + 1)
        return jnp.stack([one, total - one])
    lengths = jnp.asarray(split_up(number_of, total, reach, lean), jnp.int32)
    twos = (number_of - 1) // 2
    source_of, sink = lengths[1:1 + 2 * twos:2], lengths[2:2 + 2 * twos:2]
    margin = jnp.minimum(source_of - 1, reach - sink)
    moved = jax.random.randint(jax.random.fold_in(own_key, 1), (twos,), 0, 1 << 20) % (margin + 1)
    lengths = lengths.at[1:1 + 2 * twos:2].set(source_of - moved).at[2:2 + 2 * twos:2].set(sink + moved)
    return lengths[jax.random.permutation(jax.random.fold_in(own_key, 2), number_of)]


def bell_draw(own_key, dims, spread, reach, cuts=(), kind=jnp.bfloat16):
    values = spread * jax.random.normal(own_key, dims, jnp.float32)
    if cuts:
        values = values * levels(own_key, dims, cuts, -0.22, 0.18)
    return jnp.clip(values, -reach, reach).astype(kind)


def setup_inputs(seed: int = 0) -> dict:
    key_of = jax.random.split(jax.random.key(seed), 5)
    return {
        "start_block": draw_start_block(jax.random.fold_in(key_of[4], 71), 0),
        "block_values": bell_draw(key_of[1], (N_ROW, N_COL, NNZ, BLK, BLK), (2 * N_COL * BLK_MEAN * BLK) ** -0.5, 0.109375, ((0, 8), (1, 4))),
        "block_columns": plant(jax.random.randint(key_of[2], (N_ROW, N_COL, NNZ), 0, NCOLB), jax.random.fold_in(key_of[2], 1), 0, NCOLB - 1).astype(jnp.int32),
        "block_counts": jax.vmap(lambda own: ragged(own, NROWB, NNZ, MOST, 2))(jax.random.split(key_of[3], N_ROW * N_COL)).reshape((N_ROW, N_COL, NROWB)).astype(jnp.int32),
    }


def block_rows_of(counts, block_total):
    row_ends = jnp.cumsum(counts).astype(jnp.int32)
    positions = jnp.arange(block_total, dtype=jnp.int32)
    return jnp.sum((row_ends[None, :] <= positions[:, None]).astype(jnp.int32), axis=1)


def forward_tile(values, columns, block_row, source, row_blocks):
    vector_count = source.shape[0]
    block_size = values.shape[1]
    pieces = source.reshape(vector_count, -1, block_size)[:, columns, :]
    products = jnp.einsum("bij,kbj->kbi", values, pieces, precision=lax.Precision.HIGHEST)
    row_hot = (block_row[:, None] == jnp.arange(row_blocks, dtype=jnp.int32)[None, :]).astype(jnp.float32)
    summed = jnp.einsum("kbi,br->kri", products, row_hot, precision=lax.Precision.HIGHEST)
    return summed.reshape(vector_count, row_blocks * block_size)


def transpose_tile(values, columns, block_row, source, col_blocks):
    vector_count = source.shape[0]
    block_size = values.shape[1]
    pieces = source.reshape(vector_count, -1, block_size)[:, block_row, :]
    products = jnp.einsum("bji,kbj->kbi", values, pieces, precision=lax.Precision.HIGHEST)
    col_hot = (columns[:, None] == jnp.arange(col_blocks, dtype=jnp.int32)[None, :]).astype(jnp.float32)
    summed = jnp.einsum("kbi,bc->kci", products, col_hot, precision=lax.Precision.HIGHEST)
    return summed.reshape(vector_count, col_blocks * block_size)


def reference(start_block, block_values, block_columns, block_counts):
    row_width = STATES // N_ROW
    col_width = STATES // N_COL

    def apply_operator(source):
        def tile_step(accumulated, tile_index):
            row_slot = tile_index // N_COL
            col_slot = tile_index % N_COL
            values = block_values[row_slot, col_slot].astype(jnp.float32)
            columns = block_columns[row_slot, col_slot]
            block_row = block_rows_of(block_counts[row_slot, col_slot], NNZ)
            col_part = lax.dynamic_slice_in_dim(source, col_slot * col_width, col_width, 1).astype(jnp.float32)
            row_part = lax.dynamic_slice_in_dim(source, row_slot * row_width, row_width, 1).astype(jnp.float32)
            forward = forward_tile(values, columns, block_row, col_part, row_width // BLK)
            backward = transpose_tile(values, columns, block_row, row_part, col_width // BLK)
            current = lax.dynamic_slice_in_dim(accumulated, row_slot * row_width, row_width, 1)
            accumulated = lax.dynamic_update_slice_in_dim(accumulated, current + forward, row_slot * row_width, 1)
            current = lax.dynamic_slice_in_dim(accumulated, col_slot * col_width, col_width, 1)
            accumulated = lax.dynamic_update_slice_in_dim(accumulated, current + backward, col_slot * col_width, 1)
            return accumulated, None

        start = jnp.zeros((K, STATES), jnp.float32)
        accumulated, _ = lax.scan(tile_step, start, jnp.arange(N_ROW * N_COL, dtype=jnp.int32))
        return accumulated.astype(jnp.bfloat16)

    applied_once = apply_operator(start_block)
    applied_twice = apply_operator(applied_once)
    first_f = start_block.astype(jnp.float32)
    second_f = applied_once.astype(jnp.float32)
    third_f = applied_twice.astype(jnp.float32)

    def inner_products(left_block, right_block):
        return jnp.dot(left_block, right_block.T, precision=lax.Precision.HIGHEST)

    gram_xx = inner_products(first_f, first_f)
    gram_xy = inner_products(first_f, second_f)
    gram_yy = inner_products(second_f, second_f)
    gram_yz = inner_products(second_f, third_f)
    norm_scale = 1.0 / STATES
    basis_gram = jnp.concatenate([jnp.concatenate([gram_xx, gram_xy], 1), jnp.concatenate([gram_xy.T, gram_yy], 1)], 0) * norm_scale
    projected_gram = jnp.concatenate([jnp.concatenate([gram_xy, gram_yy], 1), jnp.concatenate([gram_yy, gram_yz], 1)], 0) * norm_scale
    return (applied_once, applied_twice, basis_gram, projected_gram)
```

```python
import jax
import jax.numpy as jnp
from jax import lax
from jax.sharding import PartitionSpec as P

highest = lax.Precision.HIGHEST
both = ("row", "col")


def block_rows_of(counts, block_total):
    positions = jnp.arange(block_total, dtype=jnp.int32)
    row_blocks = counts.shape[0]
    row_ends = [counts[0]]
    for index in range(1, row_blocks):
        row_ends.append(row_ends[-1] + counts[index])
    return sum((end <= positions).astype(jnp.int32) for end in row_ends)


def forward_tile(values, columns, block_row, source, row_blocks):
    vector_count = source.shape[0]
    block_size = values.shape[1]
    pieces = source.reshape(vector_count, -1, block_size)[:, columns, :]
    products = jnp.einsum("bij,kbj->kbi", values, pieces, preferred_element_type=jnp.float32)
    row_hot = (block_row[:, None] == jnp.arange(row_blocks, dtype=jnp.int32)[None, :]).astype(
        jnp.float32
    )
    summed = jnp.einsum("kbi,br->kri", products, row_hot, precision=highest)
    return summed.reshape(vector_count, row_blocks * block_size)


def transpose_tile(values, columns, block_row, source, col_blocks):
    vector_count = source.shape[0]
    block_size = values.shape[1]
    pieces = source.reshape(vector_count, -1, block_size)[:, block_row, :]
    products = jnp.einsum("bji,kbj->kbi", values, pieces, preferred_element_type=jnp.float32)
    col_hot = (columns[:, None] == jnp.arange(col_blocks, dtype=jnp.int32)[None, :]).astype(
        jnp.float32
    )
    summed = jnp.einsum("kbi,bc->kci", products, col_hot, precision=highest)
    return summed.reshape(vector_count, col_blocks * block_size)


def inner_products(left_block, right_block):
    return lax.dot_general(
        left_block,
        right_block,
        (((1,), (1,)), ((), ())),
        precision=highest,
        preferred_element_type=jnp.float32,
    )


def to_plane_of(col_count, ratio):
    pairs = []
    for column in range(col_count):
        planes = sorted(range(col_count), key=lambda a: -abs(a - column))
        places = sorted(range(col_count), key=lambda c: bin(c ^ column).count("1"))
        for plane, place in zip(planes, places):
            for turn in range(ratio):
                source = (plane * ratio + turn) * col_count + column
                target = (column * ratio + turn) * col_count + place
                pairs.append((source, target))
    return pairs


def xor_sum(value, others):
    level = [value, *others]
    while len(level) > 1:
        level = [level[i] + level[i + 1] for i in range(0, len(level), 2)]
    return level[0]


def local(start_block, block_values, block_columns, block_counts):
    row_count, col_count = lax.axis_size("row"), lax.axis_size("col")
    ratio = row_count // col_count
    values = block_values[0, 0]
    columns = block_columns[0, 0]
    counts = block_counts[0, 0]
    block_size = values.shape[1]
    row_blocks = counts.shape[0]
    row_width = row_blocks * block_size
    col_blocks = start_block.shape[1] // block_size
    block_row = block_rows_of(counts, values.shape[0])
    turn = lax.axis_index("row") % ratio
    norm_scale = 1.0 / (row_width * row_count)
    gather_pairs = to_plane_of(col_count, ratio)
    spread_pairs = [(target, source) for source, target in gather_pairs]
    few = col_count <= 8

    def own_part(vectors, which):
        return lax.dynamic_slice_in_dim(vectors, which * row_width, row_width, 1)

    def row_swap(value, step):
        return lax.ppermute(value, "row", [(i, i ^ step) for i in range(row_count)])

    def chip_sum(backward):
        total = own_part(backward, turn)
        for step in range(1, ratio):
            total = total + row_swap(own_part(backward, turn ^ step), step)
        return total

    def col_sum(value):
        if not few:
            return lax.psum(value, "col")
        return xor_sum(
            value,
            [
                lax.ppermute(value, "col", [(i, i ^ step) for i in range(col_count)])
                for step in range(1, col_count)
            ],
        )

    def plane_sum(value):
        if not few:
            return lax.psum(value, "row") * (1.0 / ratio)
        return xor_sum(
            value,
            [
                lax.ppermute(value, "row", [(i, i ^ (ratio * step)) for i in range(row_count)])
                for step in range(1, col_count)
            ],
        )

    start_part = own_part(start_block, turn)
    start_rows = lax.ppermute(start_part, both, gather_pairs)
    forward = forward_tile(values, columns, block_row, start_block, row_blocks)
    backward = chip_sum(transpose_tile(values, columns, block_row, start_rows, col_blocks))
    term = forward + lax.ppermute(backward, both, gather_pairs)
    applied_once = col_sum(term).astype(jnp.bfloat16)

    once_part = lax.ppermute(applied_once, both, spread_pairs)
    backward = chip_sum(transpose_tile(values, columns, block_row, applied_once, col_blocks))
    backward_term = lax.ppermute(backward, both, gather_pairs)
    grams = jnp.concatenate(
        [
            inner_products(start_part, start_part),
            inner_products(start_part, once_part),
            inner_products(once_part, once_part),
            inner_products(backward, once_part.astype(jnp.float32)),
        ],
        axis=1,
    )
    parts = [once_part] + [row_swap(once_part, step) for step in range(1, ratio)]
    for step in range(1, ratio):
        grams = grams + row_swap(grams, step)
    once_columns = jnp.concatenate(
        [
            lax.switch(turn ^ place, [lambda part=part: part for part in parts])
            if ratio > 2
            else (parts[0] if ratio == 1 else jnp.where(turn == place, parts[0], parts[1]))
            for place in range(ratio)
        ],
        axis=1,
    )
    vector_count = start_block.shape[0]
    cross = plane_sum(grams[:, 3 * vector_count :])
    grams = jnp.concatenate([grams[:, : 3 * vector_count], cross], axis=1)
    forward = forward_tile(values, columns, block_row, once_columns, row_blocks)
    message = jnp.concatenate([forward + backward_term, grams], axis=1)
    message = col_sum(message)
    applied_twice = message[:, :row_width].astype(jnp.bfloat16)
    gram_xx, gram_xy, gram_yy, cross = jnp.split(message[:, row_width:], 4, axis=1)
    gram_yz = cross + cross.T
    basis_gram = (
        jnp.concatenate(
            [jnp.concatenate([gram_xx, gram_xy], 1), jnp.concatenate([gram_xy.T, gram_yy], 1)], 0
        )
        * norm_scale
    )
    projected_gram = (
        jnp.concatenate(
            [jnp.concatenate([gram_xy, gram_yy], 1), jnp.concatenate([gram_yy, gram_yz], 1)], 0
        )
        * norm_scale
    )
    return (applied_once, applied_twice, basis_gram, projected_gram)


def solution(mesh):
    return jax.shard_map(
        local,
        mesh=mesh,
        in_specs=(
            P(None, "col"),
            P("row", "col", None, None, None),
            P("row", "col", None),
            P("row", "col", None),
        ),
        out_specs=(P(None, "row"), P(None, "row"), P(), P()),
        check_vma=False,
    )
```

```python
import functools

import jax
import jax.numpy as jnp
from jax import lax
from jax.experimental import pallas as pl
from jax.experimental.pallas import tpu as pltpu
from jax.sharding import PartitionSpec as P

highest = lax.Precision.HIGHEST
both = ("row", "col")
f32 = jnp.float32
vmem = pl.BlockSpec(memory_space=pltpu.VMEM)
smem = pl.BlockSpec(memory_space=pltpu.SMEM)


def call(kernel, out_shape, in_specs, scratch=(), flops=0, bytes_accessed=0):
    room = 2 * bytes_accessed + (1 << 20)
    return pl.pallas_call(
        kernel,
        out_shape=out_shape,
        in_specs=in_specs,
        out_specs=jax.tree.map(lambda _: vmem, out_shape),
        scratch_shapes=scratch,
        compiler_params=pltpu.CompilerParams(vmem_limit_bytes=room),
        cost_estimate=pl.CostEstimate(
            flops=flops, bytes_accessed=bytes_accessed, transcendentals=0
        ),
    )


def each_block(columns_ref, counts_ref, block_total, visit):
    row_blocks = counts_ref.shape[0]
    if block_total <= 16:
        ends = [counts_ref[0]]
        for index in range(1, row_blocks - 1):
            ends.append(ends[-1] + counts_ref[index])
        for block in range(block_total):
            visit(block, sum((block >= end).astype(jnp.int32) for end in ends), columns_ref[block])
        return

    def step(block, carry):
        row, end = carry
        later = block >= end
        row = row + later.astype(jnp.int32)
        end = end + jnp.where(later, counts_ref[row], 0)
        visit(block, row, columns_ref[block])
        return row, end

    lax.fori_loop(0, block_total, step, (jnp.int32(0), counts_ref[0]))


def split_into(pieces_ref, source, start=0):
    size = pieces_ref.shape[2]
    for index in range(source.shape[1] // size):
        pieces_ref[start + index] = source[:, index * size : (index + 1) * size]


def run_forward(columns_ref, counts_ref, values_ref, pieces, sums):
    sums[...] = jnp.zeros_like(sums)

    def visit(block, row, column):
        sums[row] += lax.dot_general(
            pieces[column],
            values_ref[block],
            (((1,), (1,)), ((), ())),
            preferred_element_type=f32,
        )

    each_block(columns_ref, counts_ref, values_ref.shape[0], visit)


def run_backward(columns_ref, counts_ref, values_ref, pieces, sums, base):
    sums[...] = jnp.zeros_like(sums)

    def visit(block, row, column):
        sums[column] += jnp.dot(
            pieces[base + row], values_ref[block], preferred_element_type=f32
        )

    each_block(columns_ref, counts_ref, values_ref.shape[0], visit)


def forward_kernel(columns_ref, counts_ref, source_ref, values_ref, out_ref, pieces, sums):
    split_into(pieces, source_ref[...])
    run_forward(columns_ref, counts_ref, values_ref, pieces, sums)
    size = sums.shape[2]
    for row in range(sums.shape[0]):
        out_ref[:, row * size : (row + 1) * size] = sums[row]


def backward_kernel(
    ratio, columns_ref, counts_ref, turn_ref, source_ref, values_ref, *rest
):
    outs, (pieces, sums) = rest[:ratio], rest[ratio:]
    turn = turn_ref[0]
    row_blocks = counts_ref.shape[0]
    whole = source_ref.shape[1] == sums.shape[0] * sums.shape[2]
    split_into(pieces, source_ref[...])
    base = turn * row_blocks if whole and ratio > 1 else 0
    run_backward(columns_ref, counts_ref, values_ref, pieces, sums, base)
    size = sums.shape[2]
    for step, out_ref in enumerate(outs):
        first = jnp.bitwise_xor(turn, step) * row_blocks
        for row in range(row_blocks):
            out_ref[:, row * size : (row + 1) * size] = sums[first + row]


def gram_kernel(ratio, scale, turn_ref, start_ref, once_ref, backward_ref, out_ref):
    width = once_ref.shape[1]
    vectors = once_ref.shape[0]
    start = start_ref[:, :width]
    for place in range(1, ratio):
        start = jnp.where(
            turn_ref[0] == place, start_ref[:, place * width : (place + 1) * width], start
        )
    once = once_ref[...]
    contract = (((1,), (1,)), ((), ()))
    gram = functools.partial(lax.dot_general, dimension_numbers=contract)
    basis = jnp.concatenate([start, once], axis=0)
    square = gram(basis, basis, preferred_element_type=f32) * scale
    wide = once.astype(f32)
    backward = backward_ref[...]
    cross = gram(wide, backward, precision=highest, preferred_element_type=f32)
    cross = cross + gram(backward, wide, precision=highest, preferred_element_type=f32)
    out_ref[:, :width] = wide
    out_ref[:, width:] = jnp.zeros((vectors, out_ref.shape[1] - width), f32)
    out_ref[:, width : width + 2 * vectors] = square[:vectors]
    out_ref[:, width + 2 * vectors : width + 4 * vectors] = square[vectors:]
    out_ref[:, width + 4 * vectors : width + 5 * vectors] = cross


def second_kernel(
    ratio, columns_ref, counts_ref, turn_ref, values_ref, *rest
):
    parts, (out_ref, pieces, sums) = rest[:ratio], rest[ratio:]
    turn = turn_ref[0]
    row_blocks = counts_ref.shape[0]
    size = sums.shape[2]
    for step, part_ref in enumerate(parts):
        first = jnp.bitwise_xor(turn, step) * row_blocks
        for row in range(row_blocks):
            pieces[first + row] = part_ref[:, row * size : (row + 1) * size].astype(pieces.dtype)
    run_forward(columns_ref, counts_ref, values_ref, pieces, sums)
    for row in range(row_blocks):
        out_ref[:, row * size : (row + 1) * size] = sums[row]


def last_kernel(norm_scale, *refs):
    messages, (twice_ref, basis_ref, projected_ref) = refs[:-3], refs[-3:]
    width = twice_ref.shape[1]
    vectors = twice_ref.shape[0]
    total = xor_sum(messages[0][...], [message[...] for message in messages[1:]])
    twice_ref[...] = total[:, :width].astype(twice_ref.dtype)
    grams = total[:, width:] * norm_scale

    def tile(index, count=1):
        return grams[:, index * vectors : (index + count) * vectors]

    basis_ref[:vectors] = tile(0, 2)
    basis_ref[vectors:] = tile(2, 2)
    projected_ref[:vectors, :vectors] = tile(1)
    projected_ref[:vectors, vectors:] = tile(3)
    projected_ref[vectors:] = tile(3, 2)


def to_plane_of(col_count, ratio):
    pairs = []
    for column in range(col_count):
        planes = sorted(range(col_count), key=lambda a: -abs(a - column))
        places = sorted(range(col_count), key=lambda c: bin(c ^ column).count("1"))
        for plane, place in zip(planes, places):
            for turn in range(ratio):
                source = (plane * ratio + turn) * col_count + column
                target = (column * ratio + turn) * col_count + place
                pairs.append((source, target))
    return pairs


def xor_sum(value, others):
    level = [value, *others]
    while len(level) > 1:
        level = [level[i] + level[i + 1] for i in range(0, len(level), 2)]
    return level[0]


def local(start_block, block_values, block_columns, block_counts):
    row_count, col_count = lax.axis_size("row"), lax.axis_size("col")
    ratio = row_count // col_count
    values = block_values[0, 0]
    columns = block_columns[0, 0]
    counts = block_counts[0, 0]
    block_total, block_size = values.shape[:2]
    row_blocks = counts.shape[0]
    row_width = row_blocks * block_size
    vectors, col_width = start_block.shape
    col_blocks = col_width // block_size
    turn = (lax.axis_index("row") % ratio).reshape(1)
    norm_scale = 1.0 / (row_width * row_count)
    gather_pairs = to_plane_of(col_count, ratio)
    spread_pairs = [(target, source) for source, target in gather_pairs]
    few = col_count <= 8
    flops = 2 * vectors * block_total * block_size**2
    bytes_accessed = 2 * block_total * block_size**2
    slab = jax.ShapeDtypeStruct((vectors, row_width), f32)

    def row_swap(value, step):
        return lax.ppermute(value, "row", [(i, i ^ step) for i in range(row_count)])

    def col_others(value):
        return [
            lax.ppermute(value, "col", [(i, i ^ step) for i in range(col_count)])
            for step in range(1, col_count)
        ]

    def plane_sum(value):
        if not few:
            return lax.psum(value, "row") * (1.0 / ratio)
        return xor_sum(value, [row_swap(value, ratio * step) for step in range(1, col_count)])

    def backward_of(source):
        outs = call(
            functools.partial(backward_kernel, ratio),
            [slab] * ratio,
            [smem, smem, smem, vmem, vmem],
            [
                pltpu.VMEM((source.shape[1] // block_size, vectors, block_size), source.dtype),
                pltpu.VMEM((col_blocks, vectors, block_size), f32),
            ],
            flops,
            bytes_accessed,
        )(columns, counts, turn, source, values)
        total = outs[0]
        for step in range(1, ratio):
            total = total + row_swap(outs[step], step)
        return total

    product_scratch = [
        pltpu.VMEM((col_blocks, vectors, block_size), start_block.dtype),
        pltpu.VMEM((row_blocks, vectors, block_size), f32),
    ]
    start_rows = lax.ppermute(start_block, both, gather_pairs)
    forward = call(
        forward_kernel, slab, [smem, smem, vmem, vmem], product_scratch, flops, bytes_accessed
    )(columns, counts, start_block, values)
    backward = backward_of(start_rows)
    term = forward + lax.ppermute(backward, both, gather_pairs)
    if few:
        applied_once = xor_sum(term, col_others(term)).astype(jnp.bfloat16)
    else:
        applied_once = lax.psum(term, "col").astype(jnp.bfloat16)

    once_part = lax.ppermute(applied_once, both, spread_pairs)
    backward = backward_of(applied_once)
    backward_term = lax.ppermute(backward, both, gather_pairs)
    message = call(
        functools.partial(gram_kernel, ratio, 1.0 / col_count),
        jax.ShapeDtypeStruct((vectors, row_width + 128), f32),
        [smem, vmem, vmem, vmem],
        (),
        8 * vectors * vectors * row_width,
        8 * vectors * row_width,
    )(turn, start_block, once_part, backward)
    messages = [message] + [row_swap(message, step) for step in range(1, ratio)]
    grams = plane_sum(sum(part[:, row_width:] for part in messages))
    forward = call(
        functools.partial(second_kernel, ratio),
        slab,
        [smem, smem, smem, vmem] + [vmem] * ratio,
        product_scratch,
        flops,
        bytes_accessed,
    )(columns, counts, turn, values, *messages)
    message = jnp.concatenate([forward + backward_term, grams], axis=1)
    others = col_others(message) if few else []
    if not few:
        message = lax.psum(message, "col")
    small = jax.ShapeDtypeStruct((2 * vectors, 2 * vectors), f32)
    applied_twice, basis_gram, projected_gram = call(
        functools.partial(last_kernel, norm_scale),
        [jax.ShapeDtypeStruct((vectors, row_width), jnp.bfloat16), small, small],
        [vmem] * (1 + len(others)),
    )(message, *others)
    return (applied_once, applied_twice, basis_gram, projected_gram)


def solution(mesh):
    return jax.shard_map(
        local,
        mesh=mesh,
        in_specs=(
            P(None, "col"),
            P("row", "col", None, None, None),
            P("row", "col", None),
            P("row", "col", None),
        ),
        out_specs=(P(None, "row"), P(None, "row"), P(), P()),
        check_vma=False,
    )
```

```python
import functools

import jax
import jax.numpy as jnp
from jax import lax
from jax.experimental import pallas as pl
from jax.experimental.pallas import tpu as pltpu
from jax.sharding import PartitionSpec as P

highest = lax.Precision.HIGHEST
both = ("row", "col")
f32 = jnp.float32
vmem = pl.BlockSpec(memory_space=pltpu.VMEM)
smem = pl.BlockSpec(memory_space=pltpu.SMEM)


def call(kernel, out_shape, in_specs, scratch=(), flops=0, bytes_accessed=0):
    room = 2 * bytes_accessed + (1 << 20)
    return pl.pallas_call(
        kernel,
        out_shape=out_shape,
        in_specs=in_specs,
        out_specs=jax.tree.map(lambda _: vmem, out_shape),
        scratch_shapes=scratch,
        compiler_params=pltpu.CompilerParams(vmem_limit_bytes=room),
        cost_estimate=pl.CostEstimate(
            flops=flops, bytes_accessed=bytes_accessed, transcendentals=0
        ),
    )


def products(columns_ref, counts_ref, values_ref, first_row, product, sums, into):
    row_blocks = counts_ref.shape[0]
    block_total = values_ref.shape[0]
    if block_total <= 16:
        ends = [counts_ref[0]]
        for index in range(1, row_blocks - 1):
            ends.append(ends[-1] + counts_ref[index])
        found = []
        for block in range(block_total):
            row = first_row + sum((block >= end).astype(jnp.int32) for end in ends)
            column = columns_ref[block]
            found.append((into(row, column), product(values_ref[block], row, column)))
        for place, value in found:
            sums[place] += value
        return

    def step(block, carry):
        row, end = carry
        later = block >= end
        row = jnp.minimum(row + later.astype(jnp.int32), row_blocks - 1)
        end = end + jnp.where(later, counts_ref[row], 0)
        column = columns_ref[block]
        place = into(first_row + row, column)
        sums[place] += product(values_ref[block], first_row + row, column)
        return row, end

    lax.fori_loop(0, block_total, step, (jnp.int32(0), counts_ref[0]))


def split_into(pieces, source_ref):
    size = pieces.shape[2]
    for index in range(pieces.shape[0]):
        pieces[index] = source_ref[:, index * size : (index + 1) * size]


def forward_kernel(columns_ref, counts_ref, values_ref, source_ref, *refs):
    term_refs, (out_ref, pieces, sums) = refs[:-3], refs[-3:]
    split_into(pieces, source_ref)
    if term_refs:
        split_into(sums, term_refs[0])
    else:
        sums[...] = jnp.zeros_like(sums)

    def product(block, row, column):
        return lax.dot_general(
            pieces[column], block, (((1,), (1,)), ((), ())), preferred_element_type=f32
        )

    products(columns_ref, counts_ref, values_ref, 0, product, sums, lambda row, column: row)
    size = sums.shape[2]
    for index in range(sums.shape[0]):
        out_ref[:, index * size : (index + 1) * size] = sums[index]


def backward_kernel(tiles, mask, turn_ref, *refs):
    columns, counts, values = refs[:tiles], refs[tiles : 2 * tiles], refs[2 * tiles : 3 * tiles]
    source_ref, *out_refs = refs[3 * tiles : -2]
    pieces, sums = refs[-2:]
    size = sums.shape[3]
    row_blocks = counts[0].shape[0]
    split_into(pieces, source_ref)
    sums[...] = jnp.zeros_like(sums)

    def product(block, row, column):
        return jnp.dot(pieces[row], block, preferred_element_type=f32)

    for tile in range(tiles):
        products(
            columns[tile],
            counts[tile],
            values[tile],
            jnp.bitwise_xor(turn_ref[0], tile) * row_blocks,
            product,
            sums.at[tile],
            lambda row, column: column,
        )

    def total(index):
        return xor_sum(sums[0, index], [sums[tile, index] for tile in range(1, tiles)])

    first = jnp.bitwise_xor(turn_ref[0], mask) * row_blocks
    for index in range(row_blocks):
        out_refs[0][:, index * size : (index + 1) * size] = total(first + index)
    for out_ref in out_refs[1:]:
        for index in range(sums.shape[1]):
            out_ref[:, index * size : (index + 1) * size] = total(index)


def gram_kernel(scale, start_ref, once_ref, backward_ref, out_ref):
    vectors = once_ref.shape[0]
    once = once_ref[...]
    gram = functools.partial(
        lax.dot_general,
        dimension_numbers=(((1,), (1,)), ((), ())),
        preferred_element_type=f32,
    )
    basis = jnp.concatenate([start_ref[...], once], axis=0)
    square = gram(basis, basis) * scale
    wide = once.astype(f32)
    backward = backward_ref[...]
    cross = gram(wide, backward, precision=highest) + gram(backward, wide, precision=highest)
    out_ref[...] = jnp.zeros_like(out_ref)
    out_ref[:, : 2 * vectors] = square[:vectors]
    out_ref[:, 2 * vectors : 4 * vectors] = square[vectors:]
    out_ref[:, 4 * vectors : 5 * vectors] = cross


def last_kernel(norm_scale, total_ref, twice_ref, basis_ref, projected_ref):
    vectors, width = twice_ref.shape
    twice_ref[...] = total_ref[:, :width].astype(twice_ref.dtype)
    grams = total_ref[:, width:] * norm_scale

    def tile(index, count=1):
        return grams[:, index * vectors : (index + count) * vectors]

    basis_ref[:vectors] = tile(0, 2)
    basis_ref[vectors:] = tile(2, 2)
    projected_ref[:vectors, :vectors] = tile(1)
    projected_ref[:vectors, vectors:] = tile(3)
    projected_ref[vectors:] = tile(3, 2)


def to_plane_of(col_count):
    pairs = []
    for column in range(col_count):
        planes = sorted(range(col_count), key=lambda a: -abs(a - column))
        places = sorted(range(col_count), key=lambda c: bin(c ^ column).count("1"))
        pairs += [((plane, column), (column, place)) for plane, place in zip(planes, places)]
    return pairs


def xor_sum(value, others):
    level = [value, *others]
    while len(level) > 1:
        level = [level[i] + level[i + 1] for i in range(0, len(level), 2)]
    return level[0]


def local(start_block, block_values, block_columns, block_counts):
    row_count, col_count = lax.axis_size("row"), lax.axis_size("col")
    ratio = row_count // col_count
    values = block_values[0, 0]
    columns = block_columns[0, 0]
    counts = block_counts[0, 0]
    block_total, block_size = values.shape[:2]
    row_blocks = counts.shape[0]
    row_width = row_blocks * block_size
    vectors, col_width = start_block.shape
    col_blocks = col_width // block_size
    turn = lax.axis_index("row") % ratio
    norm_scale = 1.0 / (row_width * row_count)
    few = col_count <= 8
    crossed = few and ratio > 1
    grid = range(col_count)
    chips = [(plane, column) for plane in grid for column in grid]
    opposite = ratio - 1

    def send(value, pairs, mask=opposite):
        def device(plane, column, member):
            return (plane * ratio + member) * col_count + column

        return lax.ppermute(
            value,
            both,
            [
                (device(*source, member), device(*target, member ^ mask))
                for source, target in pairs
                for member in range(ratio)
            ],
        )

    gather_pairs = to_plane_of(col_count)
    spread_pairs = [(target, source) for source, target in gather_pairs]
    stay = [(chip, chip) for chip in chips]

    def of_chip(value):
        return [value] + [send(value, stay, step) for step in range(1, ratio)]

    def col_sum(value):
        if not few:
            return lax.psum(value, "col")
        mask = opposite if crossed else 0
        own = send(value, stay, mask) if crossed else value
        steps = range(1, col_count)
        return xor_sum(
            own, [send(value, [((a, c), (a, c ^ step)) for a, c in chips], mask) for step in steps]
        )

    def plane_sum(value):
        if not few:
            return lax.psum(value, "row") * (1.0 / ratio)
        steps = range(1, col_count)
        return xor_sum(
            value, [send(value, [((a, c), (a ^ step, c)) for a, c in chips]) for step in steps]
        )

    def whole_slab(part):
        parts = of_chip(part)
        slab = []
        for place in range(ratio):
            piece = parts[0]
            for step in range(1, ratio):
                piece = jnp.where(turn == (place ^ step), parts[step], piece)
            slab.append(piece)
        return jnp.concatenate(slab, axis=1)

    tiles = [of_chip(columns), of_chip(counts), of_chip(values)]
    flops = 2 * vectors * block_total * block_size**2
    bytes_accessed = 2 * block_total * block_size**2
    part_shape = jax.ShapeDtypeStruct((vectors, row_width), f32)
    slab_shape = jax.ShapeDtypeStruct((vectors, col_width), f32)
    pieces = pltpu.VMEM((col_blocks, vectors, block_size), start_block.dtype)

    def forward_of(source, *term):
        tile = [arrays[opposite if crossed else 0] for arrays in tiles]
        return call(
            forward_kernel,
            part_shape,
            [smem] * 2 + [vmem] * (2 + len(term)),
            [pieces, pltpu.VMEM((row_blocks, vectors, block_size), f32)],
            flops,
            bytes_accessed,
        )(*tile, source, *term)

    def backward_of(source, outputs):
        return call(
            functools.partial(backward_kernel, ratio, 0 if crossed else opposite),
            [part_shape, slab_shape][:outputs],
            [smem] * (2 * ratio + 1) + [vmem] * (ratio + 1),
            [pieces, pltpu.VMEM((ratio, col_blocks, vectors, block_size), f32)],
            ratio * flops,
            ratio * bytes_accessed,
        )(turn.reshape(1), *tiles[0], *tiles[1], *tiles[2], source)

    start_rows = send(start_block, gather_pairs)
    forward = forward_of(start_block)
    start_rows, forward = lax.optimization_barrier((start_rows, forward))
    backward = send(backward_of(start_rows, 1)[0], gather_pairs)
    applied_once = col_sum(forward + backward).astype(jnp.bfloat16)

    once = whole_slab(applied_once)
    once_columns = send(once, spread_pairs)
    backward, backward_whole = backward_of(once, 2)
    backward = send(backward, gather_pairs)
    grams = call(
        functools.partial(gram_kernel, 1.0 / col_count),
        jax.ShapeDtypeStruct((vectors, 128), f32),
        [vmem] * 3,
        (),
        8 * vectors * vectors * col_width,
        8 * vectors * col_width,
    )(start_block, once_columns, backward_whole)
    grams = plane_sum(grams)
    total = col_sum(jnp.concatenate([forward_of(once_columns, backward), grams], axis=1))
    small = jax.ShapeDtypeStruct((2 * vectors, 2 * vectors), f32)
    applied_twice, basis_gram, projected_gram = call(
        functools.partial(last_kernel, norm_scale),
        [jax.ShapeDtypeStruct((vectors, row_width), jnp.bfloat16), small, small],
        [vmem],
    )(total)
    return (applied_once, applied_twice, basis_gram, projected_gram)


def solution(mesh):
    return jax.shard_map(
        local,
        mesh=mesh,
        in_specs=(
            P(None, "col"),
            P("row", "col", None, None, None),
            P("row", "col", None),
            P("row", "col", None),
        ),
        out_specs=(P(None, "row"), P(None, "row"), P(), P()),
        check_vma=False,
    )
```

```python
import functools

import jax
import jax.numpy as jnp
from jax import lax
from jax.experimental import pallas as pl
from jax.experimental.pallas import tpu as pltpu
from jax.sharding import PartitionSpec as P

highest = lax.Precision.HIGHEST
both = ("row", "col")
f32 = jnp.float32
vmem = pl.BlockSpec(memory_space=pltpu.VMEM)
smem = pl.BlockSpec(memory_space=pltpu.SMEM)


def call(kernel, out_shape, in_specs, scratch=(), flops=0, bytes_accessed=0):
    room = 2 * bytes_accessed + (1 << 20)
    return pl.pallas_call(
        kernel,
        out_shape=out_shape,
        in_specs=in_specs,
        out_specs=jax.tree.map(lambda _: vmem, out_shape),
        scratch_shapes=scratch,
        compiler_params=pltpu.CompilerParams(vmem_limit_bytes=room),
        cost_estimate=pl.CostEstimate(
            flops=flops, bytes_accessed=bytes_accessed, transcendentals=0
        ),
    )


def products(columns_ref, counts_ref, values_ref, first_row, product, sums, into):
    block_total = values_ref.shape[0]
    if not in_smem(block_total):
        columns, counts = columns_ref[...], counts_ref[...]
        ends = [counts[0, 0]]
        for index in range(1, counts.shape[1] - 1):
            ends.append(ends[-1] + counts[0, index])
        found = []
        for block in range(block_total):
            row = first_row + sum((block >= end).astype(jnp.int32) for end in ends)
            column = columns[0, block]
            found.append((into(row, column), product(values_ref[block], row, column)))
        for place, value in found:
            sums[place] += value
        return

    def step(block, carry):
        row, end = carry
        later = block >= end
        row = jnp.minimum(row + later.astype(jnp.int32), counts_ref.shape[1] - 1)
        end = end + jnp.where(later, counts_ref[0, row], 0)
        column = columns_ref[0, block]
        place = into(first_row + row, column)
        sums[place] += product(values_ref[block], first_row + row, column)
        return row, end

    lax.fori_loop(0, block_total, step, (jnp.int32(0), counts_ref[0, 0]))


def in_smem(block_total):
    return block_total > 16


def split_into(pieces, source_ref):
    size = pieces.shape[2]
    for index in range(pieces.shape[0]):
        pieces[index] = source_ref[:, index * size : (index + 1) * size]


def forward_kernel(columns_ref, counts_ref, values_ref, source_ref, *refs):
    term_refs, (out_ref, pieces, sums) = refs[:-3], refs[-3:]
    split_into(pieces, source_ref)
    if term_refs:
        split_into(sums, term_refs[0])
    else:
        sums[...] = jnp.zeros_like(sums)

    def product(block, row, column):
        return lax.dot_general(
            pieces[column], block, (((1,), (1,)), ((), ())), preferred_element_type=f32
        )

    products(columns_ref, counts_ref, values_ref, 0, product, sums, lambda row, column: row)
    size = sums.shape[2]
    for index in range(sums.shape[0]):
        out_ref[:, index * size : (index + 1) * size] = sums[index]


def backward_kernel(tiles, mask, *refs):
    columns, counts, values = refs[:tiles], refs[tiles : 2 * tiles], refs[2 * tiles : 3 * tiles]
    source_ref, *out_refs = refs[3 * tiles : -2]
    pieces, sums = refs[-2:]
    size = sums.shape[3]
    row_blocks = counts[0].shape[1]
    turn = lax.axis_index("row") % tiles
    split_into(pieces, source_ref)
    sums[...] = jnp.zeros_like(sums)

    def product(block, row, column):
        return jnp.dot(pieces[row], block, preferred_element_type=f32)

    for tile in range(tiles):
        products(
            columns[tile],
            counts[tile],
            values[tile],
            jnp.bitwise_xor(turn, tile) * row_blocks,
            product,
            sums.at[tile],
            lambda row, column: column,
        )

    def total(index):
        return xor_sum(sums[0, index], [sums[tile, index] for tile in range(1, tiles)])

    first = jnp.bitwise_xor(turn, mask) * row_blocks
    for index in range(row_blocks):
        out_refs[0][:, index * size : (index + 1) * size] = total(first + index)
    for out_ref in out_refs[1:]:
        for index in range(sums.shape[1]):
            out_ref[:, index * size : (index + 1) * size] = total(index)


def gram_kernel(scale, start_ref, once_ref, backward_ref, out_ref):
    vectors = once_ref.shape[0]
    rest = backward_ref[...]
    rows = [start_ref[...], once_ref[...]]
    for _ in range(3):
        rows.append(rest.astype(jnp.bfloat16))
        rest = rest - rows[-1].astype(f32)
    basis = jnp.concatenate(rows[:2], axis=0)
    dot = functools.partial(
        lax.dot_general,
        dimension_numbers=(((1,), (1,)), ((), ())),
        preferred_element_type=f32,
    )
    gram = dot(jnp.concatenate(rows, axis=0), basis)
    square = gram[: 2 * vectors] * scale
    cross = [gram[place * vectors : (place + 1) * vectors, vectors:] for place in (2, 3, 4)]
    cross = cross[0] + (cross[1] + cross[2])
    turned = dot(rows[1], rows[2]) + (dot(rows[1], rows[3]) + dot(rows[1], rows[4]))
    out_ref[...] = jnp.zeros_like(out_ref)
    out_ref[:, : 2 * vectors] = square[:vectors]
    out_ref[:, 2 * vectors : 4 * vectors] = square[vectors:]
    out_ref[:, 4 * vectors : 5 * vectors] = cross + turned


def last_kernel(norm_scale, total_ref, twice_ref, basis_ref, projected_ref):
    vectors, width = twice_ref.shape
    twice_ref[...] = total_ref[:, :width].astype(twice_ref.dtype)
    grams = total_ref[:, width:] * norm_scale

    def tile(index, count=1):
        return grams[:, index * vectors : (index + count) * vectors]

    basis_ref[:vectors] = tile(0, 2)
    basis_ref[vectors:] = tile(2, 2)
    projected_ref[:vectors, :vectors] = tile(1)
    projected_ref[:vectors, vectors:] = tile(3)
    projected_ref[vectors:] = tile(3, 2)


def to_plane_of(col_count):
    pairs = []
    for column in range(col_count):
        planes = sorted(range(col_count), key=lambda a: -abs(a - column))
        places = sorted(range(col_count), key=lambda c: bin(c ^ column).count("1"))
        pairs += [((plane, column), (column, place)) for plane, place in zip(planes, places)]
    return pairs


def xor_sum(value, others):
    level = [value, *others]
    while len(level) > 1:
        level = [level[i] + level[i + 1] for i in range(0, len(level), 2)]
    return level[0]


def local(start_block, block_values, block_columns, block_counts):
    row_count, col_count = lax.axis_size("row"), lax.axis_size("col")
    ratio = row_count // col_count
    values = block_values[0, 0]
    columns = block_columns[0]
    counts = block_counts[0]
    block_total, block_size = values.shape[:2]
    row_blocks = counts.shape[1]
    row_width = row_blocks * block_size
    vectors, col_width = start_block.shape
    col_blocks = col_width // block_size
    turn = lax.axis_index("row") % ratio
    norm_scale = 1.0 / (row_width * row_count)
    few = col_count <= 8
    crossed = few and ratio > 1
    grid = range(col_count)
    chips = [(plane, column) for plane in grid for column in grid]
    opposite = ratio - 1

    def send(value, pairs, mask=opposite):
        def device(plane, column, member):
            return (plane * ratio + member) * col_count + column

        return lax.ppermute(
            value,
            both,
            [
                (device(*source, member), device(*target, member ^ mask))
                for source, target in pairs
                for member in range(ratio)
            ],
        )

    gather_pairs = to_plane_of(col_count)
    spread_pairs = [(target, source) for source, target in gather_pairs]
    stay = [(chip, chip) for chip in chips]

    def of_chip(value):
        return [value] + [send(value, stay, step) for step in range(1, ratio)]

    def col_sum(value):
        if not few:
            return lax.psum(value, "col")
        mask = opposite if crossed else 0
        own = send(value, stay, mask) if crossed else value
        steps = range(1, col_count)
        return xor_sum(
            own, [send(value, [((a, c), (a, c ^ step)) for a, c in chips], mask) for step in steps]
        )

    def plane_sum(value):
        if not few:
            return lax.psum(value, "row") * (1.0 / ratio)
        steps = range(1, col_count)
        return xor_sum(
            value, [send(value, [((a, c), (a ^ step, c)) for a, c in chips]) for step in steps]
        )

    def whole_slab(part):
        parts = of_chip(part)
        slab = []
        for place in range(ratio):
            piece = parts[0]
            for step in range(1, ratio):
                piece = jnp.where(turn == (place ^ step), parts[step], piece)
            slab.append(piece)
        return jnp.concatenate(slab, axis=1)

    table = smem if in_smem(block_total) else vmem
    tiles = [of_chip(columns), of_chip(counts), of_chip(values)]
    flops = 2 * vectors * block_total * block_size**2
    bytes_accessed = 2 * block_total * block_size**2
    part_shape = jax.ShapeDtypeStruct((vectors, row_width), f32)
    slab_shape = jax.ShapeDtypeStruct((vectors, col_width), f32)
    pieces = pltpu.VMEM((col_blocks, vectors, block_size), start_block.dtype)

    def forward_of(source, *term):
        tile = [arrays[opposite if crossed else 0] for arrays in tiles]
        return call(
            forward_kernel,
            part_shape,
            [table] * 2 + [vmem] * (2 + len(term)),
            [pieces, pltpu.VMEM((row_blocks, vectors, block_size), f32)],
            flops,
            bytes_accessed,
        )(*tile, source, *term)

    def backward_of(source, outputs):
        return call(
            functools.partial(backward_kernel, ratio, 0 if crossed else opposite),
            [part_shape, slab_shape][:outputs],
            [table] * (2 * ratio) + [vmem] * (ratio + 1),
            [pieces, pltpu.VMEM((ratio, col_blocks, vectors, block_size), f32)],
            ratio * flops,
            ratio * bytes_accessed,
        )(*tiles[0], *tiles[1], *tiles[2], source)

    start_rows = send(start_block, gather_pairs)
    forward = forward_of(start_block)
    start_rows, forward = lax.optimization_barrier((start_rows, forward))
    backward = send(backward_of(start_rows, 1)[0], gather_pairs)
    applied_once = col_sum(forward + backward).astype(jnp.bfloat16)

    once = whole_slab(applied_once)
    once_columns = send(once, spread_pairs)
    backward, backward_whole = backward_of(once, 2)
    backward = send(backward, gather_pairs)
    grams = call(
        functools.partial(gram_kernel, 1.0 / col_count),
        jax.ShapeDtypeStruct((vectors, 128), f32),
        [vmem] * 3,
        (),
        8 * vectors * vectors * col_width,
        8 * vectors * col_width,
    )(start_block, once_columns, backward_whole)
    grams = plane_sum(grams)
    total = col_sum(jnp.concatenate([forward_of(once_columns, backward), grams], axis=1))
    small = jax.ShapeDtypeStruct((2 * vectors, 2 * vectors), f32)
    applied_twice, basis_gram, projected_gram = call(
        functools.partial(last_kernel, norm_scale),
        [jax.ShapeDtypeStruct((vectors, row_width), jnp.bfloat16), small, small],
        [vmem],
    )(total)
    return (applied_once, applied_twice, basis_gram, projected_gram)


def solution(mesh):
    return jax.shard_map(
        local,
        mesh=mesh,
        in_specs=(
            P(None, "col"),
            P("row", "col", None, None, None),
            P("row", "col", None),
            P("row", "col", None),
        ),
        out_specs=(P(None, "row"), P(None, "row"), P(), P()),
        check_vma=False,
    )
```

```python
import functools

import jax
import jax.numpy as jnp
from jax import lax
from jax.experimental import pallas as pl
from jax.experimental.pallas import tpu as pltpu
from jax.sharding import PartitionSpec as P

highest = lax.Precision.HIGHEST
both = ("row", "col")
f32 = jnp.float32
vmem = pl.BlockSpec(memory_space=pltpu.VMEM)
smem = pl.BlockSpec(memory_space=pltpu.SMEM)


def call(kernel, out_shape, in_specs, scratch=(), flops=0, bytes_accessed=0):
    room = 2 * bytes_accessed + (1 << 20)
    return pl.pallas_call(
        kernel,
        out_shape=out_shape,
        in_specs=in_specs,
        out_specs=jax.tree.map(lambda _: vmem, out_shape),
        scratch_shapes=scratch,
        compiler_params=pltpu.CompilerParams(vmem_limit_bytes=room),
        cost_estimate=pl.CostEstimate(
            flops=flops, bytes_accessed=bytes_accessed, transcendentals=0
        ),
    )


def products(columns_ref, counts_ref, values_ref, first_row, product, sums, into):
    block_total = values_ref.shape[0]
    if not in_smem(block_total):
        columns, counts = columns_ref[...], counts_ref[...]
        ends = [counts[0, 0]]
        for index in range(1, counts.shape[1] - 1):
            ends.append(ends[-1] + counts[0, index])
        found = []
        for block in range(block_total):
            row = first_row + sum((block >= end).astype(jnp.int32) for end in ends)
            column = columns[0, block]
            found.append((into(row, column), product(values_ref[block], row, column)))
        for place, value in found:
            sums[place] += value
        return

    def step(block, carry):
        row, end = carry
        later = block >= end
        row = jnp.minimum(row + later.astype(jnp.int32), counts_ref.shape[1] - 1)
        end = end + jnp.where(later, counts_ref[0, row], 0)
        column = columns_ref[0, block]
        place = into(first_row + row, column)
        sums[place] += product(values_ref[block], first_row + row, column)
        return row, end

    lax.fori_loop(0, block_total, step, (jnp.int32(0), counts_ref[0, 0]))


def in_smem(block_total):
    return block_total > 16


def split_into(pieces, source_ref):
    size = pieces.shape[2]
    for index in range(pieces.shape[0]):
        pieces[index] = source_ref[:, index * size : (index + 1) * size]


def forward_kernel(columns_ref, counts_ref, values_ref, source_ref, out_ref, pieces, sums):
    split_into(pieces, source_ref)
    sums[...] = jnp.zeros_like(sums)

    def product(block, row, column):
        return lax.dot_general(
            pieces[column], block, (((1,), (1,)), ((), ())), preferred_element_type=f32
        )

    products(columns_ref, counts_ref, values_ref, 0, product, sums, lambda row, column: row)
    size = sums.shape[2]
    for index in range(sums.shape[0]):
        out_ref[:, index * size : (index + 1) * size] = sums[index]


def backward_kernel(tiles, mask, *refs):
    columns, counts, values = refs[:tiles], refs[tiles : 2 * tiles], refs[2 * tiles : 3 * tiles]
    source_ref, out_ref, pieces, sums = refs[3 * tiles :]
    size = sums.shape[3]
    row_blocks = counts[0].shape[1]
    turn = lax.axis_index("row") % tiles
    split_into(pieces, source_ref)
    sums[...] = jnp.zeros_like(sums)

    def product(block, row, column):
        return jnp.dot(pieces[row], block, preferred_element_type=f32)

    for tile in range(tiles):
        products(
            columns[tile],
            counts[tile],
            values[tile],
            jnp.bitwise_xor(turn, tile) * row_blocks,
            product,
            sums.at[tile],
            lambda row, column: column,
        )

    def total(index):
        return xor_sum(sums[0, index], [sums[tile, index] for tile in range(1, tiles)])

    first = 0 if mask is None else jnp.bitwise_xor(turn, mask) * row_blocks
    for index in range(out_ref.shape[1] // size):
        out_ref[:, index * size : (index + 1) * size] = total(first + index).astype(out_ref.dtype)


def merge_kernel(ratio, mask, start_ref, once_ref, forward_ref, *refs):
    terms = [term_ref[...] for term_ref in refs[:-1]]
    out_ref = refs[-1]
    vectors, width = forward_ref.shape
    start, once = start_ref[...], once_ref[...]
    dot = functools.partial(
        lax.dot_general,
        dimension_numbers=(((1,), (1,)), ((), ())),
        preferred_element_type=f32,
    )
    gram = dot(jnp.concatenate([start, once, *terms], axis=0), jnp.concatenate([start, once], axis=0))
    rows = [gram[place * vectors : (place + 1) * vectors] for place in range(2 + len(terms))]
    cross = [row[:, vectors:] for row in rows[2:]]
    turned = [dot(once, term) for term in terms]
    row, column = lax.axis_index("row"), lax.axis_index("col")
    part = (row % ratio) ^ mask
    due = row // ratio == column
    backward = jnp.zeros((vectors, width), f32)
    for place in range(ratio):
        here = [term[:, place * width : (place + 1) * width].astype(f32) for term in terms]
        backward = jnp.where(due & (part == place), xor_sum(here[0], here[1:]), backward)
    out_ref[:, :width] = forward_ref[...] + backward
    out_ref[:, width:] = jnp.zeros((vectors, out_ref.shape[1] - width), f32)
    out_ref[:, width : width + 2 * vectors] = rows[0]
    out_ref[:, width + 2 * vectors : width + 4 * vectors] = rows[1]
    out_ref[:, width + 4 * vectors : width + 5 * vectors] = xor_sum(cross[0], cross[1:]) + xor_sum(
        turned[0], turned[1:]
    )


def last_kernel(norm_scale, total_ref, twice_ref, basis_ref, projected_ref):
    vectors, width = twice_ref.shape
    twice_ref[...] = total_ref[:, :width].astype(twice_ref.dtype)
    grams = total_ref[:, width:] * norm_scale

    def tile(index, count=1):
        return grams[:, index * vectors : (index + count) * vectors]

    basis_ref[:vectors] = tile(0, 2)
    basis_ref[vectors:] = tile(2, 2)
    projected_ref[:vectors, :vectors] = tile(1)
    projected_ref[:vectors, vectors:] = tile(3)
    projected_ref[vectors:] = tile(3, 2)


def to_plane_of(col_count):
    pairs = []
    for column in range(col_count):
        planes = sorted(range(col_count), key=lambda a: -abs(a - column))
        places = sorted(range(col_count), key=lambda c: bin(c ^ column).count("1"))
        pairs += [((plane, column), (column, place)) for plane, place in zip(planes, places)]
    return pairs


def xor_sum(value, others):
    level = [value, *others]
    while len(level) > 1:
        level = [sum(level[i + 1 : i + 2], level[i]) for i in range(0, len(level), 2)]
    return level[0]


def local(start_block, block_values, block_columns, block_counts):
    row_count, col_count = lax.axis_size("row"), lax.axis_size("col")
    ratio = row_count // col_count
    values = block_values[0, 0]
    columns = block_columns[0]
    counts = block_counts[0]
    block_total, block_size = values.shape[:2]
    row_blocks = counts.shape[1]
    row_width = row_blocks * block_size
    vectors, col_width = start_block.shape
    col_blocks = col_width // block_size
    turn = lax.axis_index("row") % ratio
    norm_scale = 1.0 / (row_width * row_count)
    few = col_count <= 8
    crossed = few and ratio > 1
    grid = range(col_count)
    chips = [(plane, column) for plane in grid for column in grid]
    opposite = ratio - 1

    def send(value, pairs, mask=opposite):
        def device(plane, column, member):
            return (plane * ratio + member) * col_count + column

        return lax.ppermute(
            value,
            both,
            [
                (device(*source, member), device(*target, member ^ mask))
                for source, target in pairs
                for member in range(ratio)
            ],
        )

    gather_pairs = to_plane_of(col_count)
    spread_pairs = [(target, source) for source, target in gather_pairs]
    stay = [(chip, chip) for chip in chips]

    def of_chip(value):
        return [value] + [send(value, stay, step) for step in range(1, ratio)]

    def col_sum(value):
        if not few:
            return lax.psum(value, "col")
        mask = opposite if crossed else 0
        sums = {0: value}
        for step in range(col_count):
            if step or crossed:
                sums[step] = send(value, [((a, c), (a, c ^ step)) for a, c in chips], mask)
        order = [step ^ 1 for step in range(col_count)]
        return xor_sum(sums[order[0]], [sums[step] for step in order[1:]])

    def over_planes(value):
        if few:
            terms = {0: value}
            for step in range(1, col_count):
                terms[step] = send(value, [((a, c), (a ^ step, c)) for a, c in chips])
            return [terms[step] for step in reversed(range(col_count))]
        rest, terms = lax.psum(value, "row") * (1.0 / ratio), []
        for _ in range(3):
            terms.append(rest.astype(jnp.bfloat16))
            rest = rest - terms[-1].astype(f32)
        return terms

    def whole_slab(part):
        parts = of_chip(part)
        slab = []
        for place in range(ratio):
            piece = parts[0]
            for step in range(1, ratio):
                piece = jnp.where(turn == (place ^ step), parts[step], piece)
            slab.append(piece)
        return jnp.concatenate(slab, axis=1)

    table = smem if in_smem(block_total) else vmem
    tiles = [of_chip(columns), of_chip(counts), of_chip(values)]
    flops = 2 * vectors * block_total * block_size**2
    bytes_accessed = 2 * block_total * block_size**2
    part_shape = jax.ShapeDtypeStruct((vectors, row_width), f32)
    slab_shape = jax.ShapeDtypeStruct((vectors, col_width), jnp.bfloat16 if few else f32)
    pieces = pltpu.VMEM((col_blocks, vectors, block_size), start_block.dtype)

    def forward_of(source):
        tile = [arrays[opposite if crossed else 0] for arrays in tiles]
        return call(
            forward_kernel,
            part_shape,
            [table] * 2 + [vmem] * 2,
            [pieces, pltpu.VMEM((row_blocks, vectors, block_size), f32)],
            flops,
            bytes_accessed,
        )(*tile, source)

    def backward_of(source, out_shape, mask):
        return call(
            functools.partial(backward_kernel, ratio, mask),
            out_shape,
            [table] * (2 * ratio) + [vmem] * (ratio + 1),
            [pieces, pltpu.VMEM((ratio, col_blocks, vectors, block_size), f32)],
            ratio * flops,
            ratio * bytes_accessed,
        )(*tiles[0], *tiles[1], *tiles[2], source)

    start_rows = send(start_block, gather_pairs)
    forward = forward_of(start_block)
    start_rows, forward = lax.optimization_barrier((start_rows, forward))
    backward = backward_of(start_rows, part_shape, 0 if crossed else opposite)
    backward = send(backward, gather_pairs)
    applied_once = col_sum(forward + backward).astype(jnp.bfloat16)

    once = whole_slab(applied_once)
    once_columns = send(once, spread_pairs)
    terms = over_planes(backward_of(once, slab_shape, None))
    forward = forward_of(once_columns)
    message = call(
        functools.partial(merge_kernel, ratio, opposite if crossed else 0),
        jax.ShapeDtypeStruct((vectors, row_width + 128), f32),
        [vmem] * (3 + len(terms)),
        (),
        8 * vectors * vectors * col_width,
        8 * vectors * col_width,
    )(start_block, once_columns, forward, *terms)
    total = col_sum(message)
    small = jax.ShapeDtypeStruct((2 * vectors, 2 * vectors), f32)
    applied_twice, basis_gram, projected_gram = call(
        functools.partial(last_kernel, norm_scale),
        [jax.ShapeDtypeStruct((vectors, row_width), jnp.bfloat16), small, small],
        [vmem],
    )(total)
    return (applied_once, applied_twice, basis_gram, projected_gram)


def solution(mesh):
    return jax.shard_map(
        local,
        mesh=mesh,
        in_specs=(
            P(None, "col"),
            P("row", "col", None, None, None),
            P("row", "col", None),
            P("row", "col", None),
        ),
        out_specs=(P(None, "row"), P(None, "row"), P(), P()),
        check_vma=False,
    )
```

```python
import functools

import jax
import jax.numpy as jnp
from jax import lax
from jax.experimental import pallas as pl
from jax.experimental.pallas import tpu as pltpu
from jax.sharding import PartitionSpec as P

highest = lax.Precision.HIGHEST
both = ("row", "col")
f32 = jnp.float32
vmem = pl.BlockSpec(memory_space=pltpu.VMEM)
smem = pl.BlockSpec(memory_space=pltpu.SMEM)


def call(kernel, out_shape, in_specs, scratch=(), flops=0, bytes_accessed=0):
    room = 2 * bytes_accessed + (1 << 20)
    return pl.pallas_call(
        kernel,
        out_shape=out_shape,
        in_specs=in_specs,
        out_specs=jax.tree.map(lambda _: vmem, out_shape),
        scratch_shapes=scratch,
        compiler_params=pltpu.CompilerParams(vmem_limit_bytes=room),
        cost_estimate=pl.CostEstimate(
            flops=flops, bytes_accessed=bytes_accessed, transcendentals=0
        ),
    )


def products(columns_ref, counts_ref, values_ref, first_row, product, sums, into):
    block_total = values_ref.shape[0]
    if not in_smem(block_total):
        columns, counts = columns_ref[...], counts_ref[...]
        ends = [counts[0, 0]]
        for index in range(1, counts.shape[1] - 1):
            ends.append(ends[-1] + counts[0, index])
        found = []
        for block in range(block_total):
            row = first_row + sum((block >= end).astype(jnp.int32) for end in ends)
            column = columns[0, block]
            found.append((into(row, column), product(values_ref[block], row, column)))
        for place, value in found:
            sums[place] += value
        return

    def step(block, carry):
        row, end = carry
        later = block >= end
        row = jnp.minimum(row + later.astype(jnp.int32), counts_ref.shape[1] - 1)
        end = end + jnp.where(later, counts_ref[0, row], 0)
        column = columns_ref[0, block]
        place = into(first_row + row, column)
        sums[place] += product(values_ref[block], first_row + row, column)
        return row, end

    lax.fori_loop(0, block_total, step, (jnp.int32(0), counts_ref[0, 0]))


def in_smem(block_total):
    return block_total > 16


def split_into(pieces, source_ref):
    size = pieces.shape[2]
    for index in range(pieces.shape[0]):
        pieces[index] = source_ref[:, index * size : (index + 1) * size]


def forward_kernel(columns_ref, counts_ref, values_ref, source_ref, out_ref, pieces, sums):
    split_into(pieces, source_ref)
    sums[...] = jnp.zeros_like(sums)

    def product(block, row, column):
        return lax.dot_general(
            pieces[column], block, (((1,), (1,)), ((), ())), preferred_element_type=f32
        )

    products(columns_ref, counts_ref, values_ref, 0, product, sums, lambda row, column: row)
    size = sums.shape[2]
    for index in range(sums.shape[0]):
        out_ref[:, index * size : (index + 1) * size] = sums[index]


def backward_kernel(tiles, mask, *refs):
    columns, counts, values = refs[:tiles], refs[tiles : 2 * tiles], refs[2 * tiles : 3 * tiles]
    source_ref, out_ref, pieces, sums = refs[3 * tiles :]
    size = sums.shape[3]
    row_blocks = counts[0].shape[1]
    turn = lax.axis_index("row") % tiles
    split_into(pieces, source_ref)
    sums[...] = jnp.zeros_like(sums)

    def product(block, row, column):
        return jnp.dot(pieces[row], block, preferred_element_type=f32)

    for tile in range(tiles):
        products(
            columns[tile],
            counts[tile],
            values[tile],
            jnp.bitwise_xor(turn, tile) * row_blocks,
            product,
            sums.at[tile],
            lambda row, column: column,
        )

    def total(index):
        return xor_sum(sums[0, index], [sums[tile, index] for tile in range(1, tiles)])

    first = 0 if mask is None else jnp.bitwise_xor(turn, mask) * row_blocks
    for index in range(out_ref.shape[1] // size):
        out_ref[:, index * size : (index + 1) * size] = total(first + index).astype(out_ref.dtype)


def one_backward_kernel(columns_ref, counts_ref, values_ref, source_ref, *refs):
    others, (out_ref, pieces, sums) = refs[:-3], refs[-3:]
    size = sums.shape[2]
    split_into(pieces, source_ref)
    sums[...] = jnp.zeros_like(sums)

    def product(block, row, column):
        return jnp.dot(pieces[row], block, preferred_element_type=f32)

    products(
        columns_ref, counts_ref, values_ref, 0, product, sums, lambda row, column: column
    )
    for index in range(sums.shape[0]):
        place = slice(index * size, (index + 1) * size)
        total = sums[index]
        for other_ref in others:
            total = other_ref[:, place] + total
        out_ref[:, place] = total.astype(out_ref.dtype)


def merge_kernel(ratio, mask, start_ref, once_ref, forward_ref, *refs):
    terms = [term_ref[...] for term_ref in refs[:-1]]
    out_ref = refs[-1]
    vectors, width = forward_ref.shape
    start, once = start_ref[...], once_ref[...]
    dot = functools.partial(
        lax.dot_general,
        dimension_numbers=(((1,), (1,)), ((), ())),
        preferred_element_type=f32,
    )
    wide = [term.astype(f32) for term in terms]
    whole = xor_sum(wide[0], wide[1:])
    high = whole.astype(jnp.bfloat16)
    low = (whole - high.astype(f32)).astype(jnp.bfloat16)
    gram = dot(
        jnp.concatenate([start, once, high, low], axis=0), jnp.concatenate([start, once], axis=0)
    )
    rows = [gram[place * vectors : (place + 1) * vectors] for place in range(4)]
    cross = rows[2][:, vectors:] + rows[3][:, vectors:]
    turned = dot(once, high) + dot(once, low)
    row, column = lax.axis_index("row"), lax.axis_index("col")
    part = (row % ratio) ^ mask
    due = row // ratio == column
    backward = jnp.zeros((vectors, width), f32)
    for place in range(ratio):
        here = whole[:, place * width : (place + 1) * width]
        backward = jnp.where(due & (part == place), here, backward)
    out_ref[:, :width] = forward_ref[...] + backward
    out_ref[:, width:] = jnp.zeros((vectors, out_ref.shape[1] - width), f32)
    out_ref[:, width : width + 2 * vectors] = rows[0]
    out_ref[:, width + 2 * vectors : width + 4 * vectors] = rows[1]
    out_ref[:, width + 4 * vectors : width + 5 * vectors] = cross + turned


def last_kernel(norm_scale, total_ref, twice_ref, basis_ref, projected_ref):
    vectors, width = twice_ref.shape
    twice_ref[...] = total_ref[:, :width].astype(twice_ref.dtype)
    grams = total_ref[:, width:] * norm_scale

    def tile(index, count=1):
        return grams[:, index * vectors : (index + count) * vectors]

    basis_ref[:vectors] = tile(0, 2)
    basis_ref[vectors:] = tile(2, 2)
    projected_ref[:vectors, :vectors] = tile(1)
    projected_ref[:vectors, vectors:] = tile(3)
    projected_ref[vectors:] = tile(3, 2)


def to_plane_of(col_count):
    pairs = []
    for column in range(col_count):
        planes = sorted(range(col_count), key=lambda a: -abs(a - column))
        places = sorted(range(col_count), key=lambda c: bin(c ^ column).count("1"))
        pairs += [((plane, column), (column, place)) for plane, place in zip(planes, places)]
    return pairs


def xor_sum(value, others):
    level = [value, *others]
    while len(level) > 1:
        level = [sum(level[i + 1 : i + 2], level[i]) for i in range(0, len(level), 2)]
    return level[0]


def local(start_block, block_values, block_columns, block_counts):
    row_count, col_count = lax.axis_size("row"), lax.axis_size("col")
    ratio = row_count // col_count
    values = block_values[0, 0]
    columns = block_columns[0]
    counts = block_counts[0]
    block_total, block_size = values.shape[:2]
    row_blocks = counts.shape[1]
    row_width = row_blocks * block_size
    vectors, col_width = start_block.shape
    col_blocks = col_width // block_size
    turn = lax.axis_index("row") % ratio
    norm_scale = 1.0 / (row_width * row_count)
    few = col_count <= 8
    crossed = few and ratio > 1
    grid = range(col_count)
    chips = [(plane, column) for plane in grid for column in grid]
    opposite = ratio - 1

    def send(value, pairs, mask=opposite):
        def device(plane, column, member):
            return (plane * ratio + member) * col_count + column

        return lax.ppermute(
            value,
            both,
            [
                (device(*source, member), device(*target, member ^ mask))
                for source, target in pairs
                for member in range(ratio)
            ],
        )

    gather_pairs = to_plane_of(col_count)
    spread_pairs = [(target, source) for source, target in gather_pairs]
    stay = [(chip, chip) for chip in chips]

    def of_chip(value):
        return [value] + [send(value, stay, step) for step in range(1, ratio)]

    def col_sum(value):
        if not few:
            return lax.psum(value, "col")
        mask = opposite if crossed else 0
        sums = {0: value}
        for step in range(col_count):
            if step or crossed:
                sums[step] = send(value, [((a, c), (a, c ^ step)) for a, c in chips], mask)
        order = list(range(col_count))
        return xor_sum(sums[order[0]], [sums[step] for step in order[1:]])

    def over_planes(value):
        if few:
            terms = {0: value}
            for step in range(1, col_count):
                terms[step] = send(value, [((a, c), (a ^ step, c)) for a, c in chips])
            return [terms[step] for step in range(col_count)]
        rest, terms = lax.psum(value, "row") * (1.0 / ratio), []
        for _ in range(3):
            terms.append(rest.astype(jnp.bfloat16))
            rest = rest - terms[-1].astype(f32)
        return terms

    def whole_slab(parts):
        slab = []
        for place in range(ratio):
            piece = parts[0]
            for step in range(1, ratio):
                piece = jnp.where(turn == (place ^ step), parts[step], piece)
            slab.append(piece)
        return jnp.concatenate(slab, axis=1)

    table = smem if in_smem(block_total) else vmem
    tiles = [of_chip(columns), of_chip(counts), of_chip(values)]
    flops = 2 * vectors * block_total * block_size**2
    bytes_accessed = 2 * block_total * block_size**2
    part_shape = jax.ShapeDtypeStruct((vectors, row_width), f32)
    slab_shape = jax.ShapeDtypeStruct((vectors, col_width), jnp.bfloat16 if few else f32)
    pieces = pltpu.VMEM((col_blocks, vectors, block_size), start_block.dtype)

    def forward_of(source):
        tile = [arrays[opposite if crossed else 0] for arrays in tiles]
        return call(
            forward_kernel,
            part_shape,
            [table] * 2 + [vmem] * 2,
            [pieces, pltpu.VMEM((row_blocks, vectors, block_size), f32)],
            flops,
            bytes_accessed,
        )(*tile, source)

    def backward_of(source, out_shape, mask):
        return call(
            functools.partial(backward_kernel, ratio, mask),
            out_shape,
            [table] * (2 * ratio) + [vmem] * (ratio + 1),
            [pieces, pltpu.VMEM((ratio, col_blocks, vectors, block_size), f32)],
            ratio * flops,
            ratio * bytes_accessed,
        )(*tiles[0], *tiles[1], *tiles[2], source)

    def backward_by_tile(parts):
        total = []
        for step, part in enumerate(parts):
            out_dtype = slab_shape.dtype if step == ratio - 1 else f32
            total = [
                call(
                    one_backward_kernel,
                    jax.ShapeDtypeStruct((vectors, col_width), out_dtype),
                    [table] * 2 + [vmem] * (2 + len(total)),
                    [
                        pltpu.VMEM((row_blocks, vectors, block_size), part.dtype),
                        pltpu.VMEM((col_blocks, vectors, block_size), f32),
                    ],
                    flops,
                    bytes_accessed,
                )(*[arrays[step] for arrays in tiles], part, *total)
            ]
        return total[0]

    start_rows = send(start_block, gather_pairs)
    forward = forward_of(start_block)
    start_rows, forward = lax.optimization_barrier((start_rows, forward))
    backward = backward_of(start_rows, part_shape, 0 if crossed else opposite)
    backward = send(backward, gather_pairs)
    applied_once = col_sum(forward + backward).astype(jnp.bfloat16)

    once_parts = of_chip(applied_once)
    once = whole_slab(once_parts)
    once_columns = send(once, spread_pairs)
    terms = over_planes(backward_by_tile(once_parts))
    forward = forward_of(once_columns)
    message = call(
        functools.partial(merge_kernel, ratio, opposite if crossed else 0),
        jax.ShapeDtypeStruct((vectors, row_width + 128), f32),
        [vmem] * (3 + len(terms)),
        (),
        8 * vectors * vectors * col_width,
        8 * vectors * col_width,
    )(start_block, once_columns, forward, *terms)
    total = col_sum(message)
    small = jax.ShapeDtypeStruct((2 * vectors, 2 * vectors), f32)
    applied_twice, basis_gram, projected_gram = call(
        functools.partial(last_kernel, norm_scale),
        [jax.ShapeDtypeStruct((vectors, row_width), jnp.bfloat16), small, small],
        [vmem],
    )(total)
    return (applied_once, applied_twice, basis_gram, projected_gram)


def solution(mesh):
    return jax.shard_map(
        local,
        mesh=mesh,
        in_specs=(
            P(None, "col"),
            P("row", "col", None, None, None),
            P("row", "col", None),
            P("row", "col", None),
        ),
        out_specs=(P(None, "row"), P(None, "row"), P(), P()),
        check_vma=False,
    )
```

```python
import functools

import jax
import jax.numpy as jnp
from jax import lax
from jax.experimental import pallas as pl
from jax.experimental.pallas import tpu as pltpu
from jax.sharding import PartitionSpec as P

highest = lax.Precision.HIGHEST
both = ("row", "col")
f32 = jnp.float32
vmem = pl.BlockSpec(memory_space=pltpu.VMEM)
smem = pl.BlockSpec(memory_space=pltpu.SMEM)


def call(kernel, out_shape, in_specs, scratch=(), flops=0, bytes_accessed=0):
    room = 2 * bytes_accessed + (1 << 20)
    return pl.pallas_call(
        kernel,
        out_shape=out_shape,
        in_specs=in_specs,
        out_specs=jax.tree.map(lambda _: vmem, out_shape),
        scratch_shapes=scratch,
        compiler_params=pltpu.CompilerParams(vmem_limit_bytes=room),
        cost_estimate=pl.CostEstimate(
            flops=flops, bytes_accessed=bytes_accessed, transcendentals=0
        ),
    )


def products(columns_ref, counts_ref, values_ref, first_row, product, sums, into):
    block_total = values_ref.shape[0]
    if not in_smem(block_total):
        columns, counts = columns_ref[...], counts_ref[...]
        ends = [counts[0, 0]]
        for index in range(1, counts.shape[1] - 1):
            ends.append(ends[-1] + counts[0, index])
        found = []
        for block in range(block_total):
            row = first_row + sum((block >= end).astype(jnp.int32) for end in ends)
            column = columns[0, block]
            found.append((into(row, column), product(values_ref[block], row, column)))
        for place, value in found:
            sums[place] += value
        return

    def step(block, carry):
        row, end = carry
        later = block >= end
        row = jnp.minimum(row + later.astype(jnp.int32), counts_ref.shape[1] - 1)
        end = end + jnp.where(later, counts_ref[0, row], 0)
        column = columns_ref[0, block]
        place = into(first_row + row, column)
        sums[place] += product(values_ref[block], first_row + row, column)
        return row, end

    lax.fori_loop(0, block_total, step, (jnp.int32(0), counts_ref[0, 0]))


def in_smem(block_total):
    return block_total > 16


def split_into(pieces, source_ref):
    size = pieces.shape[2]
    for index in range(pieces.shape[0]):
        pieces[index] = source_ref[:, index * size : (index + 1) * size]


def forward_kernel(columns_ref, counts_ref, values_ref, source_ref, out_ref, pieces, sums):
    split_into(pieces, source_ref)
    sums[...] = jnp.zeros_like(sums)

    def product(block, row, column):
        return lax.dot_general(
            pieces[column], block, (((1,), (1,)), ((), ())), preferred_element_type=f32
        )

    products(columns_ref, counts_ref, values_ref, 0, product, sums, lambda row, column: row)
    size = sums.shape[2]
    for index in range(sums.shape[0]):
        out_ref[:, index * size : (index + 1) * size] = sums[index]


def backward_kernel(tiles, mask, *refs):
    columns, counts, values = refs[:tiles], refs[tiles : 2 * tiles], refs[2 * tiles : 3 * tiles]
    source_ref, out_ref, pieces, sums = refs[3 * tiles :]
    size = sums.shape[3]
    row_blocks = counts[0].shape[1]
    turn = lax.axis_index("row") % tiles
    split_into(pieces, source_ref)
    sums[...] = jnp.zeros_like(sums)

    def product(block, row, column):
        return jnp.dot(pieces[row], block, preferred_element_type=f32)

    for tile in range(tiles):
        products(
            columns[tile],
            counts[tile],
            values[tile],
            jnp.bitwise_xor(turn, tile) * row_blocks,
            product,
            sums.at[tile],
            lambda row, column: column,
        )

    def total(index):
        return xor_sum(sums[0, index], [sums[tile, index] for tile in range(1, tiles)])

    first = 0 if mask is None else jnp.bitwise_xor(turn, mask) * row_blocks
    for index in range(out_ref.shape[1] // size):
        out_ref[:, index * size : (index + 1) * size] = total(first + index).astype(out_ref.dtype)


def one_backward_kernel(columns_ref, counts_ref, values_ref, source_ref, *refs):
    others, (out_ref, pieces, sums) = refs[:-3], refs[-3:]
    size = sums.shape[2]
    split_into(pieces, source_ref)
    sums[...] = jnp.zeros_like(sums)

    def product(block, row, column):
        return jnp.dot(pieces[row], block, preferred_element_type=f32)

    products(
        columns_ref, counts_ref, values_ref, 0, product, sums, lambda row, column: column
    )
    for index in range(sums.shape[0]):
        place = slice(index * size, (index + 1) * size)
        total = sums[index]
        for other_ref in others:
            total = other_ref[:, place] + total
        out_ref[:, place] = total.astype(out_ref.dtype)


def merge_kernel(ratio, mask, start_ref, once_ref, forward_ref, *refs):
    terms = [term_ref[...] for term_ref in refs[:-1]]
    out_ref = refs[-1]
    vectors, width = forward_ref.shape
    start, once = start_ref[...], once_ref[...]
    dot = functools.partial(
        lax.dot_general,
        dimension_numbers=(((1,), (1,)), ((), ())),
        preferred_element_type=f32,
    )
    wide = [term.astype(f32) for term in terms]
    whole = xor_sum(wide[0], wide[1:])
    high = whole.astype(jnp.bfloat16)
    low = (whole - high.astype(f32)).astype(jnp.bfloat16)
    gram = dot(
        jnp.concatenate([start, once, high, low], axis=0), jnp.concatenate([start, once], axis=0)
    )
    rows = [gram[place * vectors : (place + 1) * vectors] for place in range(4)]
    cross = rows[2][:, vectors:] + rows[3][:, vectors:]
    turned = dot(once, high) + dot(once, low)
    row, column = lax.axis_index("row"), lax.axis_index("col")
    part = (row % ratio) ^ mask
    due = row // ratio == column
    backward = jnp.zeros((vectors, width), f32)
    for place in range(ratio):
        here = whole[:, place * width : (place + 1) * width]
        backward = jnp.where(due & (part == place), here, backward)
    out_ref[:, :width] = forward_ref[...] + backward
    out_ref[:, width:] = jnp.zeros((vectors, out_ref.shape[1] - width), f32)
    out_ref[:, width : width + 2 * vectors] = rows[0]
    out_ref[:, width + 2 * vectors : width + 4 * vectors] = rows[1]
    out_ref[:, width + 4 * vectors : width + 5 * vectors] = cross + turned


def last_kernel(norm_scale, total_ref, twice_ref, basis_ref, projected_ref):
    vectors, width = twice_ref.shape
    twice_ref[...] = total_ref[:, :width].astype(twice_ref.dtype)
    grams = total_ref[:, width:] * norm_scale

    def tile(index, count=1):
        return grams[:, index * vectors : (index + count) * vectors]

    basis_ref[:vectors] = tile(0, 2)
    basis_ref[vectors:] = tile(2, 2)
    projected_ref[:vectors, :vectors] = tile(1)
    projected_ref[:vectors, vectors:] = tile(3)
    projected_ref[vectors:] = tile(3, 2)


def to_plane_of(col_count):
    pairs = []
    for column in range(col_count):
        planes = sorted(range(col_count), key=lambda a: -abs(a - column))
        places = sorted(range(col_count), key=lambda c: (bin(c ^ column).count("1"), c ^ column))
        pairs += [((plane, column), (column, place)) for plane, place in zip(planes, places)]
    return pairs


def xor_sum(value, others):
    level = [value, *others]
    while len(level) > 1:
        level = [sum(level[i + 1 : i + 2], level[i]) for i in range(0, len(level), 2)]
    return level[0]


def local(start_block, block_values, block_columns, block_counts):
    row_count, col_count = lax.axis_size("row"), lax.axis_size("col")
    ratio = row_count // col_count
    values = block_values[0, 0]
    columns = block_columns[0]
    counts = block_counts[0]
    block_total, block_size = values.shape[:2]
    row_blocks = counts.shape[1]
    row_width = row_blocks * block_size
    vectors, col_width = start_block.shape
    col_blocks = col_width // block_size
    turn = lax.axis_index("row") % ratio
    norm_scale = 1.0 / (row_width * row_count)
    few = col_count <= 8
    crossed = few and ratio > 1
    grid = range(col_count)
    chips = [(plane, column) for plane in grid for column in grid]
    opposite = ratio - 1

    def send(value, pairs, mask=opposite):
        def device(plane, column, member):
            return (plane * ratio + member) * col_count + column

        return lax.ppermute(
            value,
            both,
            [
                (device(*source, member), device(*target, member ^ mask))
                for source, target in pairs
                for member in range(ratio)
            ],
        )

    gather_pairs = to_plane_of(col_count)
    spread_pairs = [(target, source) for source, target in gather_pairs]
    stay = [(chip, chip) for chip in chips]

    def of_chip(value):
        return [value] + [send(value, stay, step) for step in range(1, ratio)]

    def col_sum(value):
        if not few:
            return lax.psum(value, "col")
        mask = opposite if crossed else 0
        sums = {0: value}
        for step in range(col_count):
            if step or crossed:
                sums[step] = send(value, [((a, c), (a, c ^ step)) for a, c in chips], mask)
        order = list(range(col_count))
        return xor_sum(sums[order[0]], [sums[step] for step in order[1:]])

    def over_planes(value):
        if few:
            terms = {0: value}
            for step in range(1, col_count):
                terms[step] = send(value, [((a, c), (a ^ step, c)) for a, c in chips])
            return [terms[step] for step in range(col_count)]
        rest, terms = lax.psum(value, "row") * (1.0 / ratio), []
        for _ in range(3):
            terms.append(rest.astype(jnp.bfloat16))
            rest = rest - terms[-1].astype(f32)
        return terms

    def whole_slab(parts):
        slab = []
        for place in range(ratio):
            piece = parts[0]
            for step in range(1, ratio):
                piece = jnp.where(turn == (place ^ step), parts[step], piece)
            slab.append(piece)
        return jnp.concatenate(slab, axis=1)

    table = smem if in_smem(block_total) else vmem
    tiles = [of_chip(columns), of_chip(counts), of_chip(values)]
    flops = 2 * vectors * block_total * block_size**2
    bytes_accessed = 2 * block_total * block_size**2
    part_shape = jax.ShapeDtypeStruct((vectors, row_width), f32)
    slab_shape = jax.ShapeDtypeStruct((vectors, col_width), jnp.bfloat16 if few else f32)
    pieces = pltpu.VMEM((col_blocks, vectors, block_size), start_block.dtype)

    def forward_of(source):
        tile = [arrays[opposite if crossed else 0] for arrays in tiles]
        return call(
            forward_kernel,
            part_shape,
            [table] * 2 + [vmem] * 2,
            [pieces, pltpu.VMEM((row_blocks, vectors, block_size), f32)],
            flops,
            bytes_accessed,
        )(*tile, source)

    def backward_of(source, out_shape, mask):
        return call(
            functools.partial(backward_kernel, ratio, mask),
            out_shape,
            [table] * (2 * ratio) + [vmem] * (ratio + 1),
            [pieces, pltpu.VMEM((ratio, col_blocks, vectors, block_size), f32)],
            ratio * flops,
            ratio * bytes_accessed,
        )(*tiles[0], *tiles[1], *tiles[2], source)

    def backward_by_tile(parts):
        total = []
        for step, part in enumerate(parts):
            out_dtype = slab_shape.dtype if step == ratio - 1 else f32
            total = [
                call(
                    one_backward_kernel,
                    jax.ShapeDtypeStruct((vectors, col_width), out_dtype),
                    [table] * 2 + [vmem] * (2 + len(total)),
                    [
                        pltpu.VMEM((row_blocks, vectors, block_size), part.dtype),
                        pltpu.VMEM((col_blocks, vectors, block_size), f32),
                    ],
                    flops,
                    bytes_accessed,
                )(*[arrays[step] for arrays in tiles], part, *total)
            ]
        return total[0]

    start_rows = send(start_block, gather_pairs)
    forward = forward_of(start_block)
    start_rows, forward = lax.optimization_barrier((start_rows, forward))
    backward = backward_of(start_rows, part_shape, 0 if crossed else opposite)
    backward = send(backward, gather_pairs)
    applied_once = col_sum(forward + backward).astype(jnp.bfloat16)

    once_parts = of_chip(applied_once)
    once = whole_slab(once_parts)
    once_columns = send(once, spread_pairs)
    terms = over_planes(backward_by_tile(once_parts))
    forward = forward_of(once_columns)
    message = call(
        functools.partial(merge_kernel, ratio, opposite if crossed else 0),
        jax.ShapeDtypeStruct((vectors, row_width + 128), f32),
        [vmem] * (3 + len(terms)),
        (),
        8 * vectors * vectors * col_width,
        8 * vectors * col_width,
    )(start_block, once_columns, forward, *terms)
    total = col_sum(message)
    small = jax.ShapeDtypeStruct((2 * vectors, 2 * vectors), f32)
    applied_twice, basis_gram, projected_gram = call(
        functools.partial(last_kernel, norm_scale),
        [jax.ShapeDtypeStruct((vectors, row_width), jnp.bfloat16), small, small],
        [vmem],
    )(total)
    return (applied_once, applied_twice, basis_gram, projected_gram)


def solution(mesh):
    return jax.shard_map(
        local,
        mesh=mesh,
        in_specs=(
            P(None, "col"),
            P("row", "col", None, None, None),
            P("row", "col", None),
            P("row", "col", None),
        ),
        out_specs=(P(None, "row"), P(None, "row"), P(), P()),
        check_vma=False,
    )
```

```python
import functools

import jax
import jax.numpy as jnp
from jax import lax
from jax.experimental import pallas as pl
from jax.experimental.pallas import tpu as pltpu
from jax.sharding import PartitionSpec as P

highest = lax.Precision.HIGHEST
both = ("row", "col")
f32 = jnp.float32
vmem = pl.BlockSpec(memory_space=pltpu.VMEM)
smem = pl.BlockSpec(memory_space=pltpu.SMEM)


def call(kernel, out_shape, in_specs, scratch=(), flops=0, bytes_accessed=0):
    room = 2 * bytes_accessed + (1 << 20)
    return pl.pallas_call(
        kernel,
        out_shape=out_shape,
        in_specs=in_specs,
        out_specs=jax.tree.map(lambda _: vmem, out_shape),
        scratch_shapes=scratch,
        compiler_params=pltpu.CompilerParams(vmem_limit_bytes=room),
        cost_estimate=pl.CostEstimate(
            flops=flops, bytes_accessed=bytes_accessed, transcendentals=0
        ),
    )


def products(columns_ref, counts_ref, values_ref, first_row, product, sums, into):
    block_total = values_ref.shape[0]
    if not in_smem(block_total):
        columns, counts = columns_ref[...], counts_ref[...]
        ends = [counts[0, 0]]
        for index in range(1, counts.shape[1] - 1):
            ends.append(ends[-1] + counts[0, index])
        found = []
        for block in range(block_total):
            row = first_row + sum((block >= end).astype(jnp.int32) for end in ends)
            column = columns[0, block]
            found.append((into(row, column), product(values_ref[block], row, column)))
        for place, value in found:
            sums[place] += value
        return

    def step(block, carry):
        row, end = carry
        later = block >= end
        row = jnp.minimum(row + later.astype(jnp.int32), counts_ref.shape[1] - 1)
        end = end + jnp.where(later, counts_ref[0, row], 0)
        column = columns_ref[0, block]
        place = into(first_row + row, column)
        sums[place] += product(values_ref[block], first_row + row, column)
        return row, end

    lax.fori_loop(0, block_total, step, (jnp.int32(0), counts_ref[0, 0]))


def in_smem(block_total):
    return block_total > 16


def split_into(pieces, source_ref):
    size = pieces.shape[2]
    for index in range(pieces.shape[0]):
        pieces[index] = source_ref[:, index * size : (index + 1) * size]


def forward_kernel(columns_ref, counts_ref, values_ref, source_ref, out_ref, pieces, sums):
    split_into(pieces, source_ref)
    sums[...] = jnp.zeros_like(sums)

    def product(block, row, column):
        return lax.dot_general(
            pieces[column], block, (((1,), (1,)), ((), ())), preferred_element_type=f32
        )

    products(columns_ref, counts_ref, values_ref, 0, product, sums, lambda row, column: row)
    size = sums.shape[2]
    for index in range(sums.shape[0]):
        out_ref[:, index * size : (index + 1) * size] = sums[index]


def backward_kernel(tiles, mask, *refs):
    columns, counts, values = refs[:tiles], refs[tiles : 2 * tiles], refs[2 * tiles : 3 * tiles]
    source_ref, out_ref, pieces, sums = refs[3 * tiles :]
    size = sums.shape[3]
    row_blocks = counts[0].shape[1]
    turn = lax.axis_index("row") % tiles
    split_into(pieces, source_ref)
    sums[...] = jnp.zeros_like(sums)

    def product(block, row, column):
        return jnp.dot(pieces[row], block, preferred_element_type=f32)

    for tile in range(tiles):
        products(
            columns[tile],
            counts[tile],
            values[tile],
            jnp.bitwise_xor(turn, tile) * row_blocks,
            product,
            sums.at[tile],
            lambda row, column: column,
        )

    def total(index):
        return xor_sum(sums[0, index], [sums[tile, index] for tile in range(1, tiles)])

    first = 0 if mask is None else jnp.bitwise_xor(turn, mask) * row_blocks
    for index in range(out_ref.shape[1] // size):
        out_ref[:, index * size : (index + 1) * size] = total(first + index).astype(out_ref.dtype)


def one_backward_kernel(columns_ref, counts_ref, values_ref, source_ref, *refs):
    others, (out_ref, pieces, sums) = refs[:-3], refs[-3:]
    size = sums.shape[2]
    split_into(pieces, source_ref)
    sums[...] = jnp.zeros_like(sums)

    def product(block, row, column):
        return jnp.dot(pieces[row], block, preferred_element_type=f32)

    products(
        columns_ref, counts_ref, values_ref, 0, product, sums, lambda row, column: column
    )
    for index in range(sums.shape[0]):
        place = slice(index * size, (index + 1) * size)
        total = sums[index]
        for other_ref in others:
            total = other_ref[:, place] + total
        out_ref[:, place] = total.astype(out_ref.dtype)


def merge_kernel(ratio, mask, start_ref, once_ref, forward_ref, *refs):
    terms = [term_ref[...] for term_ref in refs[:-1]]
    out_ref = refs[-1]
    vectors, width = forward_ref.shape
    start, once = start_ref[...], once_ref[...]
    dot = functools.partial(
        lax.dot_general,
        dimension_numbers=(((1,), (1,)), ((), ())),
        preferred_element_type=f32,
    )
    wide = [term.astype(f32) for term in terms]
    whole = xor_sum(wide[0], wide[1:])
    high = whole.astype(jnp.bfloat16)
    low = (whole - high.astype(f32)).astype(jnp.bfloat16)
    gram = dot(
        jnp.concatenate([start, once, high, low], axis=0), jnp.concatenate([start, once], axis=0)
    )
    rows = [gram[place * vectors : (place + 1) * vectors] for place in range(4)]
    cross = rows[2][:, vectors:] + rows[3][:, vectors:]
    turned = dot(once, high) + dot(once, low)
    row, column = lax.axis_index("row"), lax.axis_index("col")
    part = (row % ratio) ^ mask
    due = row // ratio == column
    backward = jnp.zeros((vectors, width), f32)
    for place in range(ratio):
        here = whole[:, place * width : (place + 1) * width]
        backward = jnp.where(due & (part == place), here, backward)
    out_ref[:, :width] = forward_ref[...] + backward
    out_ref[:, width:] = jnp.zeros((vectors, out_ref.shape[1] - width), f32)
    out_ref[:, width : width + 2 * vectors] = rows[0]
    out_ref[:, width + 2 * vectors : width + 4 * vectors] = rows[1]
    out_ref[:, width + 4 * vectors : width + 5 * vectors] = cross + turned


def last_kernel(norm_scale, total_ref, twice_ref, basis_ref, projected_ref):
    vectors, width = twice_ref.shape
    twice_ref[...] = total_ref[:, :width].astype(twice_ref.dtype)
    grams = total_ref[:, width:] * norm_scale

    def tile(index, count=1):
        return grams[:, index * vectors : (index + count) * vectors]

    basis_ref[:vectors] = tile(0, 2)
    basis_ref[vectors:] = tile(2, 2)
    projected_ref[:vectors, :vectors] = tile(1)
    projected_ref[:vectors, vectors:] = tile(3)
    projected_ref[vectors:] = tile(3, 2)


def to_plane_of(col_count):
    pairs = []
    for column in range(col_count):
        planes = sorted(range(col_count), key=lambda a: -abs(a - column))
        places = sorted(range(col_count), key=lambda c: (bin(c ^ column).count("1"), c ^ column))
        pairs += [((plane, column), (column, place)) for plane, place in zip(planes, places)]
    return pairs


def xor_sum(value, others):
    level = [value, *others]
    while len(level) > 1:
        level = [sum(level[i + 1 : i + 2], level[i]) for i in range(0, len(level), 2)]
    return level[0]


def local(start_block, block_values, block_columns, block_counts):
    row_count, col_count = lax.axis_size("row"), lax.axis_size("col")
    ratio = row_count // col_count
    values = block_values[0, 0]
    columns = block_columns[0]
    counts = block_counts[0]
    block_total, block_size = values.shape[:2]
    row_blocks = counts.shape[1]
    row_width = row_blocks * block_size
    vectors, col_width = start_block.shape
    col_blocks = col_width // block_size
    turn = lax.axis_index("row") % ratio
    norm_scale = 1.0 / (row_width * row_count)
    few = col_count <= 8
    crossed = few and ratio > 1
    grid = range(col_count)
    chips = [(plane, column) for plane in grid for column in grid]
    opposite = ratio - 1

    def send(value, pairs, mask=opposite):
        def device(plane, column, member):
            return (plane * ratio + member) * col_count + column

        return lax.ppermute(
            value,
            both,
            [
                (device(*source, member), device(*target, member ^ mask))
                for source, target in pairs
                for member in range(ratio)
            ],
        )

    gather_pairs = to_plane_of(col_count)
    spread_pairs = [(target, source) for source, target in gather_pairs]
    stay = [(chip, chip) for chip in chips]

    def of_chip(value):
        return [value] + [send(value, stay, step) for step in range(1, ratio)]

    def col_sum(value):
        if not few:
            return lax.psum(value, "col")
        mask = opposite if crossed else 0
        sums = {0: value}
        for step in range(col_count):
            if step or crossed:
                sums[step] = send(value, [((a, c), (a, c ^ step)) for a, c in chips], mask)
        order = list(range(col_count))
        return xor_sum(sums[order[0]], [sums[step] for step in order[1:]])

    def over_planes(value):
        if few:
            terms = {0: value}
            for step in range(1, col_count):
                terms[step] = send(value, [((a, c), (a ^ step, c)) for a, c in chips])
            return [terms[step] for step in sorted(terms, key=lambda step: (step & 1, step))]
        rest, terms = lax.psum(value, "row") * (1.0 / ratio), []
        for _ in range(3):
            terms.append(rest.astype(jnp.bfloat16))
            rest = rest - terms[-1].astype(f32)
        return terms

    def whole_slab(parts):
        slab = []
        for place in range(ratio):
            piece = parts[0]
            for step in range(1, ratio):
                piece = jnp.where(turn == (place ^ step), parts[step], piece)
            slab.append(piece)
        return jnp.concatenate(slab, axis=1)

    table = smem if in_smem(block_total) else vmem
    tiles = [of_chip(columns), of_chip(counts), of_chip(values)]
    flops = 2 * vectors * block_total * block_size**2
    bytes_accessed = 2 * block_total * block_size**2
    part_shape = jax.ShapeDtypeStruct((vectors, row_width), f32)
    slab_shape = jax.ShapeDtypeStruct((vectors, col_width), jnp.bfloat16 if few else f32)
    pieces = pltpu.VMEM((col_blocks, vectors, block_size), start_block.dtype)

    def forward_of(source):
        tile = [arrays[opposite if crossed else 0] for arrays in tiles]
        return call(
            forward_kernel,
            part_shape,
            [table] * 2 + [vmem] * 2,
            [pieces, pltpu.VMEM((row_blocks, vectors, block_size), f32)],
            flops,
            bytes_accessed,
        )(*tile, source)

    def backward_of(source, out_shape, mask):
        return call(
            functools.partial(backward_kernel, ratio, mask),
            out_shape,
            [table] * (2 * ratio) + [vmem] * (ratio + 1),
            [pieces, pltpu.VMEM((ratio, col_blocks, vectors, block_size), f32)],
            ratio * flops,
            ratio * bytes_accessed,
        )(*tiles[0], *tiles[1], *tiles[2], source)

    def backward_by_tile(parts):
        total = []
        for step, part in enumerate(parts):
            out_dtype = slab_shape.dtype if step == ratio - 1 else f32
            total = [
                call(
                    one_backward_kernel,
                    jax.ShapeDtypeStruct((vectors, col_width), out_dtype),
                    [table] * 2 + [vmem] * (2 + len(total)),
                    [
                        pltpu.VMEM((row_blocks, vectors, block_size), part.dtype),
                        pltpu.VMEM((col_blocks, vectors, block_size), f32),
                    ],
                    flops,
                    bytes_accessed,
                )(*[arrays[step] for arrays in tiles], part, *total)
            ]
        return total[0]

    start_rows = send(start_block, gather_pairs)
    forward = forward_of(start_block)
    start_rows, forward = lax.optimization_barrier((start_rows, forward))
    backward = backward_of(start_rows, part_shape, 0 if crossed else opposite)
    backward = send(backward, gather_pairs)
    applied_once = col_sum(forward + backward).astype(jnp.bfloat16)

    once_parts = of_chip(applied_once)
    once = whole_slab(once_parts)
    once_columns = send(once, spread_pairs)
    terms = over_planes(backward_by_tile(once_parts))
    forward = forward_of(once_columns)
    message = call(
        functools.partial(merge_kernel, ratio, opposite if crossed else 0),
        jax.ShapeDtypeStruct((vectors, row_width + 128), f32),
        [vmem] * (3 + len(terms)),
        (),
        8 * vectors * vectors * col_width,
        8 * vectors * col_width,
    )(start_block, once_columns, forward, *terms)
    total = col_sum(message)
    small = jax.ShapeDtypeStruct((2 * vectors, 2 * vectors), f32)
    applied_twice, basis_gram, projected_gram = call(
        functools.partial(last_kernel, norm_scale),
        [jax.ShapeDtypeStruct((vectors, row_width), jnp.bfloat16), small, small],
        [vmem],
    )(total)
    return (applied_once, applied_twice, basis_gram, projected_gram)


def solution(mesh):
    return jax.shard_map(
        local,
        mesh=mesh,
        in_specs=(
            P(None, "col"),
            P("row", "col", None, None, None),
            P("row", "col", None),
            P("row", "col", None),
        ),
        out_specs=(P(None, "row"), P(None, "row"), P(), P()),
        check_vma=False,
    )
```
